32 devices in a mesh: heads: 2 (over y), blocks: 16 (over z, x, core).
Axes of the slice: x: 2, y: 2, z: 4, core: 2. Of those that a mesh axis runs over, the one named last changes fastest.
Arguments:
- hidden: bfloat16 [128, 2048], P(None, 'blocks'), may hold values from -18 to 18
- w_query: bfloat16 [2048, 2048], P('blocks', 'heads'), may hold values from -1 to 1
- w_key: bfloat16 [2048, 2048], P('blocks', 'heads'), may hold values from -1 to 1
- w_value: bfloat16 [2048, 2048], P('blocks', 'heads'), may hold values from -0.125 to 0.125
- w_out: bfloat16 [2048, 2048], P('heads', 'blocks'), may hold values from -0.125 to 0.125
- cache_key: bfloat16 [4, 16384, 2048], P(None, 'blocks', 'heads'), may hold values from -80 to 80
- cache_value: bfloat16 [4, 16384, 2048], P(None, 'blocks', 'heads'), may hold values from -6 to 6
- parents: int32 [4, 32], replicated, may hold values from 0 to 30, as said below
- lengths: int32 [4], replicated, may hold values from 1 to 16352
- holder: int32 [4, 16], replicated, may hold values from 0 to 15, as said below
- selector: int32 [4, 32, 32], replicated, may hold values from 0 to 1, as said below
Outputs:
- mixed: bfloat16 [128, 2048], P('heads', 'blocks')
- key_out: bfloat16 [4, 16384, 2048], P(None, 'blocks', 'heads')
- value_out: bfloat16 [4, 16384, 2048], P(None, 'blocks', 'heads')
The draws below stay inside these ranges and needn't reach their ends.
Inputs may be any that keep to these rules, and one draw needn't show every extreme that they name: parents[r, 0] = 0; for i >= 1, parents[r, i] is one of the four tokens before i (never below 0). Each row is a permutation of 0 to 15; for the first 2 requests holder[r, j] = j. For each request, the first rows of selector[r] are one-hot and pick the tokens of one path from the root down the tree, row a picking the token of depth a; the other rows are zero.
All inputs are finite; a program needn't handle non-finite values.
Results may differ from the reference program's by a relative error of at most 0.012.
The reference program's roundings to bfloat16 on the way (of `block_weights`, `tree_weights`, `attended` and `fresh`) count: a program that leaves them out, or rounds other values in their place, can miss the bound.
Values may be sent and summed in bfloat16 or wider, within the bound.
No kernel may reach another device: no remote copies, remote signals or barrier semaphores. Data moves between devices by JAX's collectives and lax.ppermute only.
A program may use at most 192 MiB of HBM per device.

```python
import math
import jax
import jax.numpy as jnp
from jax import lax

D = 2048
HD = 64
ROT = 32
REQ = 4
TREE = 32
CAP = 16384
NBLK = 16


def tree_tables(key):
    tree_key = jax.random.fold_in(key, 11)
    offset_key, pick_key, end_key = jax.random.split(tree_key, 3)
    offsets = jax.random.randint(offset_key, (REQ, TREE), 1, 5)
    chosen = jax.random.randint(pick_key, (), 0, REQ)
    positions = jnp.arange(TREE, dtype=jnp.int32)
    forced = (jnp.arange(REQ, dtype=jnp.int32)[:, None] == chosen) & (positions[None, :] == TREE - 1)
    offsets = jnp.where(forced, 1, offsets)
    parents = jnp.maximum(positions[None, :] - offsets, 0).astype(jnp.int32)

    def deepen(column, depths):
        parent_col = lax.dynamic_index_in_dim(parents, column, 1, keepdims=False)
        parent_depth = jnp.take_along_axis(depths, parent_col[:, None], axis=1)[:, 0]
        return depths.at[:, column].set(parent_depth + 1)
    depths = lax.fori_loop(1, TREE, deepen, jnp.zeros((REQ, TREE), jnp.int32))
    endpoints = jax.random.randint(end_key, (REQ,), TREE // 2, TREE).astype(jnp.int32)

    def climb(column, carried):
        current, onpath = carried
        onpath = onpath | (positions[None, :] == current[:, None])
        current = jnp.take_along_axis(parents, current[:, None], axis=1)[:, 0]
        return (current, onpath)
    start_path = jnp.zeros((REQ, TREE), dtype=bool)
    unused, onpath = lax.fori_loop(0, TREE, climb, (endpoints, start_path))
    selector = (onpath[:, None, :] & (depths[:, None, :] == positions[None, :, None])).astype(jnp.int32)
    return (parents, selector)


def draw_parents(key, part):
    return tree_tables(key)[0]


def draw_selector(key, part):
    return tree_tables(key)[1]


def draw_lengths(key, part):
    length_key, pick_key = jax.random.split(jax.random.fold_in(key, 23))
    drawn = jax.random.randint(length_key, (REQ,), 1, CAP - TREE + 1)
    chosen = jax.random.randint(pick_key, (), 0, REQ)
    return jnp.where(jnp.arange(REQ, dtype=jnp.int32) == chosen, CAP - TREE, drawn).astype(jnp.int32)


def draw_holder(key, part):
    row_keys = jax.random.split(jax.random.fold_in(key, 37), REQ)

    def shuffled(row_key):
        return jax.random.permutation(row_key, NBLK).astype(jnp.int32)
    permuted = jax.vmap(shuffled)(row_keys)
    identity = jnp.broadcast_to(jnp.arange(NBLK, dtype=jnp.int32)[None, :], (REQ, NBLK))
    return jnp.where(jnp.arange(REQ, dtype=jnp.int32)[:, None] < REQ // 2, identity, permuted)


def draw_cache_key(key, part):
    base_key = jax.random.fold_in(jax.random.fold_in(key, 51), 0)
    normal = jax.random.normal(base_key, (REQ, CAP, D), jnp.float32)
    return jnp.clip(3.0 * normal, -18.0, 18.0).astype(jnp.bfloat16)


def draw_hidden(key, part):
    base_key = jax.random.fold_in(jax.random.fold_in(key, 67), 0)
    return jnp.clip(jax.random.normal(base_key, (REQ * TREE, D), jnp.float32), -6.0, 6.0).astype(jnp.bfloat16)


def draw_w_query(key, part):
    query_key = jax.random.fold_in(jax.random.fold_in(key, 79), 0)
    inverse_root = 1.0 / math.sqrt(D)
    return (jnp.clip(jax.random.normal(query_key, (D, D), jnp.float32), -4.0, 4.0) * inverse_root).astype(jnp.bfloat16)


def draw_w_key(key, part):
    other_key = jax.random.fold_in(jax.random.fold_in(key, 79), 1)
    inverse_root = 1.0 / math.sqrt(D)
    independent = jnp.clip(jax.random.normal(other_key, (D, D), jnp.float32), -4.0, 4.0)
    return (3.0 * independent * inverse_root).astype(jnp.bfloat16)


def level_of(own_key, extent, cuts, low, top_value):
    def one(position, shards_of):
        heights = jax.random.uniform(jax.random.fold_in(jax.random.fold_in(own_key, 6), position), (shards_of,), jnp.float32, low / len(cuts), top_value / len(cuts))
        return jnp.repeat(jnp.exp(heights), extent[position] // shards_of).reshape((-1,) + (1,) * (len(extent) - position - 1))

    gain = one(*cuts[0])
    for cut in cuts[1:]:
        gain = gain * one(*cut)
    return gain


def gaussian(key, extent, scale, most, shards=(), kind=jnp.bfloat16):
    values = scale * jax.random.normal(key, extent, jnp.float32)
    if shards:
        values = values * level_of(key, extent, shards, -0.22, 0.18)
    return jnp.clip(values, -most, most).astype(kind)


def setup_inputs(seed: int = 0) -> dict:
    key_of = jax.random.split(jax.random.key(seed), 12)
    return {
        "hidden": draw_hidden(jax.random.fold_in(key_of[11], 71), 0),
        "w_query": draw_w_query(jax.random.fold_in(key_of[11], 71), 0),
        "w_key": draw_w_key(jax.random.fold_in(key_of[11], 71), 0),
        "w_value": gaussian(key_of[3], (D, D), D ** -0.5, 0.125, ((0, 16), (1, 2))),
        "w_out": gaussian(key_of[4], (D, D), D ** -0.5, 0.125, ((0, 2), (1, 16))),
        "cache_key": draw_cache_key(jax.random.fold_in(key_of[11], 71), 0),
        "cache_value": gaussian(key_of[6], (REQ, CAP, D), 1.0, 6.0, ((1, 16), (2, 2))),
        "parents": draw_parents(jax.random.fold_in(key_of[11], 71), 0),
        "lengths": draw_lengths(jax.random.fold_in(key_of[11], 71), 0),
        "holder": draw_holder(jax.random.fold_in(key_of[11], 71), 0),
        "selector": draw_selector(jax.random.fold_in(key_of[11], 71), 0),
    }


masked_low = -1e+30
rotary_base = 10000.0

def ancestry(parents):
    tree_size = parents.shape[0]
    nodes = jnp.arange(tree_size, dtype=jnp.int32)
    parent_hop = ((parents[:, None] == nodes[None, :]) & (nodes[:, None] > 0)).astype(jnp.float32)
    reached = jnp.eye(tree_size, dtype=jnp.float32) + parent_hop
    for _ in range(tree_size.bit_length()):
        reached = jnp.minimum(jnp.dot(reached, reached, precision=lax.Precision.HIGHEST), 1.0)
    return reached

def rotate(values, positions):
    row_count = values.shape[0]
    shaped = values.reshape(row_count, -1, HD)
    half_rot = ROT // 2
    inverse_freq = rotary_base ** (-2.0 * jnp.arange(half_rot, dtype=jnp.float32) / ROT)
    angles = positions.astype(jnp.float32)[:, None] * inverse_freq[None, :]
    cosine = jnp.cos(angles)[:, None, :]
    sine = jnp.sin(angles)[:, None, :]
    leading = shaped[:, :, :half_rot]
    trailing = shaped[:, :, half_rot:ROT]
    turned = jnp.concatenate([leading * cosine - trailing * sine, trailing * cosine + leading * sine, shaped[:, :, ROT:]], axis=2)
    return turned.reshape(row_count, -1)

def finalize(cache_top, cache_sum, cache_out, tree_max, tree_sum, tree_out):
    joint_top = jnp.maximum(cache_top, tree_max)
    cache_scale = jnp.exp(cache_top - joint_top)
    tree_scale = jnp.exp(tree_max - joint_top)
    numerator = cache_out * cache_scale[..., None] + tree_out * tree_scale[..., None]
    denominator = cache_sum * cache_scale + tree_sum * tree_scale
    return numerator / denominator[..., None]

def reference(hidden, w_query, w_key, w_value, w_out, cache_key, cache_value, parents, lengths, holder, selector):
    requests, tree_size = parents.shape
    model_width = hidden.shape[1]
    head_count = model_width // HD
    block_count = holder.shape[1]
    block_len = cache_key.shape[1] // block_count
    scale = 1.0 / math.sqrt(HD)
    highest = lax.Precision.HIGHEST
    ancestors = jax.vmap(ancestry)(parents)
    depths = (lax.optimization_barrier(jnp.sum(ancestors, axis=2)) - 1.0).astype(jnp.int32)
    positions = (lengths[:, None].astype(jnp.int32) + depths).reshape(-1)
    queries = rotate(jnp.dot(hidden, w_query, preferred_element_type=jnp.float32), positions).astype(jnp.bfloat16)
    keys_new = rotate(jnp.dot(hidden, w_key, preferred_element_type=jnp.float32), positions).astype(jnp.bfloat16)
    values_new = jnp.dot(hidden, w_value, preferred_element_type=jnp.float32).astype(jnp.bfloat16)

    def one_request(request_items):
        query_one, key_one, value_one, cached_keys, cached_values, tree_mask, length, holder_row, selector_row = request_items
        slots = jnp.arange(block_count, dtype=jnp.int32)
        stored_logical = lax.optimization_barrier(jnp.sum(slots[None, :] * (holder_row[None, :] == slots[:, None]).astype(jnp.int32), axis=1))
        logical = stored_logical[:, None] * block_len + jnp.arange(block_len, dtype=jnp.int32)[None, :]
        live_rows = logical < length
        query_heads = query_one.astype(jnp.float32).reshape(tree_size, head_count, HD)
        key_blocks = cached_keys.astype(jnp.float32).reshape(block_count, block_len, head_count, HD)
        value_blocks = cached_values.astype(jnp.float32).reshape(block_count, block_len, head_count, HD)
        scores = jnp.einsum('ihd,nbhd->hinb', query_heads, key_blocks, precision=highest) * scale
        mask = live_rows[None, None, :, :]
        block_max = lax.optimization_barrier(jnp.max(jnp.where(mask, scores, masked_low), axis=3))
        exponent = jnp.where(mask, jnp.exp(scores - block_max[..., None]), 0.0)
        block_sum = lax.optimization_barrier(jnp.sum(exponent, axis=3))
        block_weights = lax.optimization_barrier(exponent.astype(jnp.bfloat16)).astype(jnp.float32)
        block_out = jnp.einsum('hinb,nbhd->hind', block_weights, value_blocks, precision=highest)
        cache_top = lax.optimization_barrier(jnp.max(block_max, axis=2))
        factor = jnp.exp(block_max - cache_top[..., None])
        cache_sum = lax.optimization_barrier(jnp.sum(block_sum * factor, axis=2))
        cache_out = lax.optimization_barrier(jnp.sum(block_out * factor[..., None], axis=2))
        tree_keys = key_one.astype(jnp.float32).reshape(tree_size, head_count, HD)
        tree_values = value_one.astype(jnp.float32).reshape(tree_size, head_count, HD)
        tree_scores = jnp.einsum('ihd,jhd->hij', query_heads, tree_keys, precision=highest) * scale
        tree_allowed = (tree_mask > 0.5)[None, :, :]
        tree_max = lax.optimization_barrier(jnp.max(jnp.where(tree_allowed, tree_scores, masked_low), axis=2))
        tree_exp = jnp.where(tree_allowed, jnp.exp(tree_scores - tree_max[..., None]), 0.0)
        tree_sum = lax.optimization_barrier(jnp.sum(tree_exp, axis=2))
        tree_weights = lax.optimization_barrier(tree_exp.astype(jnp.bfloat16)).astype(jnp.float32)
        tree_out = jnp.einsum('hij,jhd->hid', tree_weights, tree_values, precision=highest)
        combined = finalize(cache_top, cache_sum, cache_out, tree_max, tree_sum, tree_out)
        attended = combined.transpose(1, 0, 2).reshape(tree_size, model_width).astype(jnp.bfloat16)
        accepted = lax.optimization_barrier(jnp.sum(selector_row, axis=1)) > 0
        fresh = jnp.dot(selector_row.astype(jnp.bfloat16), jnp.concatenate([key_one, value_one], axis=1), preferred_element_type=jnp.float32).astype(jnp.bfloat16)
        offsets = logical.reshape(-1) - length
        tree_slots = jnp.arange(tree_size, dtype=jnp.int32)
        hits = (offsets[:, None] == tree_slots[None, :]) & accepted[None, :]
        written = jnp.dot(hits.astype(jnp.bfloat16), fresh, preferred_element_type=jnp.float32).astype(jnp.bfloat16)
        touched = jnp.any(hits, axis=1)[:, None]
        new_keys = jnp.where(touched, written[:, :model_width], cached_keys)
        new_values = jnp.where(touched, written[:, model_width:], cached_values)
        return (attended, new_keys, new_values)
    attended, key_out, value_out = lax.map(one_request, (queries.reshape(requests, tree_size, model_width), keys_new.reshape(requests, tree_size, model_width), values_new.reshape(requests, tree_size, model_width), cache_key, cache_value, ancestors, lengths.astype(jnp.int32), holder.astype(jnp.int32), selector))
    mixed = jnp.dot(attended.reshape(requests * tree_size, model_width), w_out, preferred_element_type=jnp.float32).astype(jnp.bfloat16)
    return (mixed, key_out, value_out)
```

```python
import functools
import math

import jax
import jax.numpy as jnp
from jax import lax
from jax.experimental import pallas as pl
from jax.experimental.pallas import tpu as pltpu
from jax.sharding import PartitionSpec as P

HD = 64
ROT = 32
LANES = 128


masked_low = -1e30
rotary_base = 10000.0


def swap(value, axis, bit):
    size = lax.axis_size(axis)
    return lax.ppermute(value, axis, [(i, i ^ bit) for i in range(size)])


def ancestry(parents):
    tree_size = parents.shape[0]
    nodes = jnp.arange(tree_size, dtype=jnp.int32)
    parent_hop = ((parents[:, None] == nodes[None, :]) & (nodes[:, None] > 0)).astype(jnp.float32)
    reached = jnp.eye(tree_size, dtype=jnp.float32) + parent_hop
    for _ in range(tree_size.bit_length()):
        reached = jnp.minimum(jnp.dot(reached, reached, precision=lax.Precision.HIGHEST), 1.0)
    return reached


def rotary_tables(positions):
    column = jnp.arange(LANES, dtype=jnp.int32) % HD
    half = ROT // 2
    exponent = (column % half).astype(jnp.float32)
    inverse_freq = rotary_base ** (-2.0 * exponent / ROT)
    angles = positions.astype(jnp.float32)[:, None] * inverse_freq[None, :]
    cosine = jnp.where(column < ROT, jnp.cos(angles), 1.0)
    sine = jnp.sin(angles)
    ahead = jnp.where(column < half, -sine, 0.0)
    behind = jnp.where((column >= half) & (column < ROT), sine, 0.0)
    return jnp.stack([cosine, ahead, behind])


def turn(chunk, tables):
    half = ROT // 2
    ahead = pltpu.roll(chunk, LANES - half, axis=1)
    behind = pltpu.roll(chunk, half, axis=1)
    return chunk * tables[0] + ahead * tables[1] + behind * tables[2]


def add_rotate_kernel(rotated_width, one_ref, two_ref, tables_ref, out_ref):
    for start in range(0, one_ref.shape[1], LANES):
        columns = slice(start, start + LANES)
        chunk = one_ref[:, columns] + two_ref[:, columns]
        if start < rotated_width:
            chunk = turn(chunk, tables_ref)
        out_ref[:, columns] = chunk.astype(out_ref.dtype)


def add_rotate(one, two, tables, rotated_width):
    return pl.pallas_call(
        functools.partial(add_rotate_kernel, rotated_width),
        out_shape=jax.ShapeDtypeStruct(one.shape, jnp.bfloat16),
        name="add_rotate",
    )(one, two, tables)


def head_of(extent, axis, shape, unit):
    return lax.broadcasted_iota(jnp.int32, shape, axis) // unit


def block_diagonal(queries, heads):
    tokens, width = queries.shape
    tall = jnp.concatenate([queries] * heads, axis=0)
    shape = (heads * tokens, width)
    row_head = lax.broadcasted_iota(jnp.int32, shape, 0) // tokens
    column_head = lax.broadcasted_iota(jnp.int32, shape, 1) // HD
    return jnp.where(row_head == column_head, tall, jnp.zeros_like(tall))


def diagonal_blocks(tall, heads, tokens):
    width = tall.shape[1]
    column_head = lax.broadcasted_iota(jnp.int32, (tokens, width), 1) // HD
    out = tall[:tokens]
    for head in range(1, heads):
        out = jnp.where(column_head == head, tall[head * tokens : (head + 1) * tokens], out)
    return out


def cache_kernel(slot, heads, scale, reqs, live, q_ref, k_ref, v_ref, out_ref, stat_ref):
    group = pl.program_id(0)
    tokens = q_ref.shape[0]
    queries = block_diagonal(q_ref[...], heads)
    keys = k_ref[0]
    values = v_ref[0]
    scores = lax.dot_general(
        queries, keys, (((1,), (1,)), ((), ())), preferred_element_type=jnp.float32
    ) * scale
    mask = lax.broadcasted_iota(jnp.int32, scores.shape, 1) < live[reqs[slot]]
    scores = jnp.where(mask, scores, masked_low)
    top = jnp.max(scores, axis=1, keepdims=True)
    exponent = jnp.where(mask, jnp.exp(scores - top), 0.0)
    total = jnp.sum(exponent, axis=1, keepdims=True)
    out = jnp.dot(exponent.astype(jnp.bfloat16), values, preferred_element_type=jnp.float32)
    out_ref[...] = diagonal_blocks(out, heads, tokens)
    lane = lax.broadcasted_iota(jnp.int32, (tokens, LANES), 1)
    stats = jnp.where(group == 0, jnp.zeros((tokens, LANES), jnp.float32), stat_ref[...])
    for head in range(heads):
        rows = slice(head * tokens, (head + 1) * tokens)
        where = group * heads + head
        stats = jnp.where(lane == where, top[rows], stats)
        stats = jnp.where(lane == where + HD, total[rows], stats)
    stat_ref[...] = stats


def cache_attention(slot, queries, cache_key, cache_value, reqs, live, scale):
    tokens, width = queries.shape
    block_len = cache_key.shape[1]
    group = min(256, width)
    heads = group // HD
    cache_spec = pl.BlockSpec((1, block_len, group), lambda g, reqs, live: (reqs[slot], 0, g))
    return pl.pallas_call(
        functools.partial(cache_kernel, slot, heads, scale),
        grid_spec=pltpu.PrefetchScalarGridSpec(
            num_scalar_prefetch=2,
            grid=(width // group,),
            in_specs=[pl.BlockSpec((tokens, group), lambda g, reqs, live: (0, g)), cache_spec, cache_spec],
            out_specs=[
                pl.BlockSpec((tokens, group), lambda g, reqs, live: (0, g)),
                pl.BlockSpec((tokens, LANES), lambda g, reqs, live: (0, 0)),
            ],
        ),
        out_shape=[
            jax.ShapeDtypeStruct((tokens, width), jnp.float32),
            jax.ShapeDtypeStruct((tokens, LANES), jnp.float32),
        ],
        cost_estimate=pl.CostEstimate(
            flops=4 * tokens * width * block_len * heads,
            transcendentals=tokens * (width // HD) * block_len,
            bytes_accessed=4 * block_len * width,
        ),
        name="cache_attention",
    )(reqs, live, queries, cache_key, cache_value)


def spread(stats, pair, shape):
    lane = lax.broadcasted_iota(jnp.int32, shape, 1)
    first = jnp.broadcast_to(stats[:, 2 * pair : 2 * pair + 1], shape)
    second = jnp.broadcast_to(stats[:, 2 * pair + 1 : 2 * pair + 2], shape)
    return jnp.where(lane < HD, first, second)


def merged_stats(one, two):
    top = jnp.maximum(one, two)
    scale_one = jnp.exp(one - top)
    scale_two = jnp.exp(two - top)
    total = one * pltpu.roll(scale_one, HD, axis=1) + two * pltpu.roll(scale_two, HD, axis=1)
    lane = lax.broadcasted_iota(jnp.int32, one.shape, 1)
    return jnp.where(lane < HD, top, total), scale_one, scale_two


def merge_kernel(width, one_ref, two_ref, out_ref):
    one = one_ref[:, width:]
    two = two_ref[:, width:]
    stats, scale_one, scale_two = merged_stats(one, two)
    out_ref[:, width:] = stats
    for pair in range(width // LANES):
        columns = slice(pair * LANES, (pair + 1) * LANES)
        shape = (one.shape[0], LANES)
        out_ref[:, columns] = one_ref[:, columns] * spread(scale_one, pair, shape) + two_ref[
            :, columns
        ] * spread(scale_two, pair, shape)


def merge(one, two, width):
    return pl.pallas_call(
        functools.partial(merge_kernel, width),
        out_shape=jax.ShapeDtypeStruct(one.shape, jnp.float32),
        name="merge",
    )(one, two)


def finish_kernel(width, heads, scale, one_ref, two_ref, q_ref, kv_ref, tree_ref, out_ref):
    tokens = q_ref.shape[0]
    stats, scale_one, scale_two = merged_stats(one_ref[:, width:], two_ref[:, width:])
    group = heads * HD
    allowed = jnp.concatenate([tree_ref[...]] * heads, axis=0) > 0.5
    lane = lax.broadcasted_iota(jnp.int32, (tokens, LANES), 1)
    tree_stats = jnp.zeros((tokens, LANES), jnp.float32)
    tree_outs = []
    for start in range(0, width, group):
        queries = block_diagonal(q_ref[:, start : start + group], heads)
        keys = kv_ref[:, start : start + group]
        values = kv_ref[:, width + start : width + start + group]
        scores = lax.dot_general(
            queries, keys, (((1,), (1,)), ((), ())), preferred_element_type=jnp.float32
        ) * scale
        scores = jnp.where(allowed, scores, masked_low)
        top = jnp.max(scores, axis=1, keepdims=True)
        exponent = jnp.where(allowed, jnp.exp(scores - top), 0.0)
        total = jnp.sum(exponent, axis=1, keepdims=True)
        out = jnp.dot(exponent.astype(jnp.bfloat16), values, preferred_element_type=jnp.float32)
        tree_outs.append(diagonal_blocks(out, heads, tokens))
        for head in range(heads):
            rows = slice(head * tokens, (head + 1) * tokens)
            where = start // HD + head
            tree_stats = jnp.where(lane == where, top[rows], tree_stats)
            tree_stats = jnp.where(lane == where + HD, total[rows], tree_stats)
    joint, scale_cache, scale_tree = merged_stats(stats, tree_stats)
    total = pltpu.roll(joint, HD, axis=1)
    for pair in range(width // LANES):
        columns = slice(pair * LANES, (pair + 1) * LANES)
        shape = (tokens, LANES)
        cached = one_ref[:, columns] * spread(scale_one, pair, shape) + two_ref[
            :, columns
        ] * spread(scale_two, pair, shape)
        start = pair * LANES
        tree = tree_outs[start // group][:, start % group : start % group + LANES]
        numerator = cached * spread(scale_cache, pair, shape) + tree * spread(scale_tree, pair, shape)
        out_ref[:, columns] = (numerator / spread(total, pair, shape)).astype(out_ref.dtype)


def finish(one, two, queries, key_value, tree, scale):
    tokens, width = queries.shape
    heads = min(256, width) // HD
    return pl.pallas_call(
        functools.partial(finish_kernel, width, heads, scale),
        out_shape=jax.ShapeDtypeStruct((tokens, width), jnp.bfloat16),
        name="finish",
    )(one, two, queries, key_value, tree)


def patch_kernel(firsts, starts, kv_ref, sel_ref, key_ref, value_ref, key_out, value_out):
    request = pl.program_id(0)
    step = pl.program_id(1)
    rows, width = key_ref.shape[1:]
    slots = sel_ref.shape[1]
    last = pl.num_programs(1) - 1
    block = firsts[request, step]
    row = lax.broadcasted_iota(jnp.int32, (rows, slots), 0) + block * rows - starts[request]
    depth = lax.broadcasted_iota(jnp.int32, (rows, slots), 1)
    hits = (row == depth).astype(jnp.bfloat16)
    picks = jnp.dot(hits, sel_ref[0], preferred_element_type=jnp.float32)
    touched = jnp.sum(picks, axis=1, keepdims=True) > 0.5
    written = jnp.dot(
        picks.astype(jnp.bfloat16), kv_ref[0], preferred_element_type=jnp.float32
    ).astype(jnp.bfloat16)
    key_out[0] = jnp.where(touched, written[:, :width], key_ref[0])
    value_out[0] = jnp.where(touched, written[:, width:], value_ref[0])


def patch(key_value, reqs, selector, firsts, starts, keys, values):
    requests, block_len, width = keys.shape
    tokens = selector.shape[1]
    rows = tokens
    cache_spec = pl.BlockSpec((1, rows, width), lambda r, s, firsts, starts: (r, firsts[r, s], 0))
    return pl.pallas_call(
        patch_kernel,
        grid_spec=pltpu.PrefetchScalarGridSpec(
            num_scalar_prefetch=2,
            grid=(requests, 2),
            in_specs=[
                pl.BlockSpec((1, tokens, 2 * width), lambda r, s, firsts, starts: (r, 0, 0)),
                pl.BlockSpec((1, tokens, tokens), lambda r, s, firsts, starts: (r, 0, 0)),
                cache_spec,
                cache_spec,
            ],
            out_specs=[cache_spec, cache_spec],
        ),
        out_shape=[jax.ShapeDtypeStruct(keys.shape, keys.dtype)] * 2,
        input_output_aliases={4: 0, 5: 1},
        cost_estimate=pl.CostEstimate(
            flops=0, transcendentals=0, bytes_accessed=16 * requests * rows * width
        ),
        name="patch",
    )(firsts, starts, key_value, selector, keys, values)


def on_device(
    hidden,
    w_query,
    w_key,
    w_value,
    w_out,
    cache_key,
    cache_value,
    parents,
    lengths,
    holder,
    selector,
):
    requests, tree_size = parents.shape
    width = w_query.shape[1]
    block_len = cache_key.shape[1]
    block_count = holder.shape[1]
    scale = 1.0 / math.sqrt(HD)
    axis = "blocks"
    index = lax.axis_index(axis)
    levels = requests.bit_length() - 1
    bits = block_count.bit_length() - 1
    assert 1 << levels == requests and 1 << bits == block_count and bits > levels
    split = [1 << s for s in range(levels)]
    whole = [1 << s for s in range(levels, bits)]
    own = sum(((index >> s) & 1) << (levels - 1 - s) for s in range(levels))
    reqs = own ^ jnp.arange(requests, dtype=jnp.int32)

    slots = jnp.arange(block_count, dtype=jnp.int32)
    logical = jnp.sum(slots[None, :] * (holder == index).astype(jnp.int32), axis=1)
    starts = lengths - logical * block_len
    live = jnp.clip(starts, 0, block_len)

    rows = jnp.take(hidden.reshape(requests, tree_size, -1), reqs, axis=0)
    rows = rows.reshape(requests * tree_size, -1)

    def scattered(weights):
        value = jnp.dot(rows, weights, preferred_element_type=jnp.float32)
        value = value.reshape(requests, tree_size, -1)
        for bit in split:
            half = value.shape[0] // 2
            value = value[:half] + swap(value[half:], axis, bit)
        value = value[0]
        for bit in whole[:-1]:
            value = value + swap(value, axis, bit)
        return value, swap(value, axis, whole[-1])

    ancestors = ancestry(lax.dynamic_index_in_dim(parents, own, 0, False))
    depths = (jnp.sum(ancestors, axis=1) - 1.0).astype(jnp.int32)
    positions = lax.dynamic_index_in_dim(lengths, own, 0, False) + depths
    tables = rotary_tables(positions)

    query_own = add_rotate(*scattered(w_query), tables, width)
    kv_own = add_rotate(*scattered(jnp.concatenate([w_key, w_value], axis=1)), tables, width)

    def gathered(value):
        value = value[None]
        for bit in reversed(split):
            value = jnp.concatenate([value, swap(value, axis, bit)], axis=0)
        return value

    queries = gathered(query_own)
    parts = [None] * requests
    for slot in reversed(range(requests)):
        out, stats = cache_attention(slot, queries[slot], cache_key, cache_value, reqs, live, scale)
        parts[slot] = jnp.concatenate([out, stats], axis=1)
    count = requests
    for bit in split:
        count //= 2
        received = swap(jnp.concatenate(parts[count:], axis=0), axis, bit)
        parts = [
            merge(parts[k], received[k * tree_size : (k + 1) * tree_size], width)
            for k in range(count)
        ]
    cached = parts[0]
    for bit in whole[:-1]:
        cached = merge(cached, swap(cached, axis, bit), width)
    other = swap(cached, axis, whole[-1])
    attended_own = finish(cached, other, query_own, kv_own, ancestors, scale)
    attended = gathered(attended_own).reshape(requests * tree_size, width)
    mixed = jnp.dot(attended, w_out, preferred_element_type=jnp.float32)
    mixed = jnp.take(mixed.reshape(requests, tree_size, -1), reqs, axis=0)
    mixed = mixed.reshape(requests * tree_size, -1)
    head_bit = lax.axis_size("heads") // 2
    while head_bit:
        high = (lax.axis_index("heads") & head_bit) > 0
        half = mixed.shape[0] // 2
        keep = jnp.where(high, mixed[half:], mixed[:half])
        send = jnp.where(high, mixed[:half], mixed[half:])
        mixed = keep + swap(send, "heads", head_bit)
        head_bit //= 2
    mixed = mixed.astype(jnp.bfloat16)

    fresh = jnp.take(gathered(kv_own), reqs, axis=0)
    tiles = block_len // tree_size
    first = lax.div(starts + block_len * block_count, jnp.int32(tree_size)) - tiles * block_count
    firsts = jnp.clip(first[:, None] + jnp.arange(2, dtype=jnp.int32)[None, :], 0, tiles - 1)
    key_out, value_out = patch(
        fresh, reqs, selector.astype(jnp.bfloat16), firsts, starts, cache_key, cache_value
    )
    return (mixed, key_out, value_out)


def solution(mesh):
    return jax.shard_map(
        on_device,
        mesh=mesh,
        in_specs=(
            P(None, "blocks"),
            P("blocks", "heads"),
            P("blocks", "heads"),
            P("blocks", "heads"),
            P("heads", "blocks"),
            P(None, "blocks", "heads"),
            P(None, "blocks", "heads"),
            P(),
            P(),
            P(),
            P(),
        ),
        out_specs=(P("heads", "blocks"), P(None, "blocks", "heads"), P(None, "blocks", "heads")),
        check_vma=False,
    )
```

```python
import functools
import math

import jax
import jax.numpy as jnp
from jax import lax
from jax.experimental import pallas as pl
from jax.experimental.pallas import tpu as pltpu
from jax.sharding import PartitionSpec as P

HD = 64
ROT = 32
LANES = 128


masked_low = -1e30
rotary_base = 10000.0


def swap(value, axis, bit):
    size = lax.axis_size(axis)
    return lax.ppermute(value, axis, [(i, i ^ bit) for i in range(size)])


def ancestry(parents):
    tree_size = parents.shape[0]
    nodes = jnp.arange(tree_size, dtype=jnp.int32)
    parent_hop = ((parents[:, None] == nodes[None, :]) & (nodes[:, None] > 0)).astype(jnp.float32)
    reached = jnp.eye(tree_size, dtype=jnp.float32) + parent_hop
    for _ in range(tree_size.bit_length()):
        reached = jnp.minimum(jnp.dot(reached, reached, precision=lax.Precision.HIGHEST), 1.0)
    return reached


def rotary_tables(positions):
    column = jnp.arange(LANES, dtype=jnp.int32) % HD
    half = ROT // 2
    exponent = (column % half).astype(jnp.float32)
    inverse_freq = rotary_base ** (-2.0 * exponent / ROT)
    angles = positions.astype(jnp.float32)[:, None] * inverse_freq[None, :]
    cosine = jnp.where(column < ROT, jnp.cos(angles), 1.0)
    sine = jnp.sin(angles)
    ahead = jnp.where(column < half, -sine, 0.0)
    behind = jnp.where((column >= half) & (column < ROT), sine, 0.0)
    return jnp.stack([cosine, ahead, behind])


def rotate(value, tables):
    half = ROT // 2
    tables = jnp.tile(tables, (1, 1, value.shape[1] // LANES))
    ahead = jnp.roll(value, -half, axis=1)
    behind = jnp.roll(value, half, axis=1)
    return value * tables[0] + ahead * tables[1] + behind * tables[2]


def block_diagonal(queries, heads):
    tokens, width = queries.shape
    tall = jnp.concatenate([queries] * heads, axis=0)
    shape = (heads * tokens, width)
    row_head = lax.broadcasted_iota(jnp.int32, shape, 0) // tokens
    column_head = lax.broadcasted_iota(jnp.int32, shape, 1) // HD
    return jnp.where(row_head == column_head, tall, jnp.zeros_like(tall))


def diagonal_blocks(tall, heads, tokens):
    width = tall.shape[1]
    column_head = lax.broadcasted_iota(jnp.int32, (tokens, width), 1) // HD
    out = tall[:tokens]
    for head in range(1, heads):
        out = jnp.where(column_head == head, tall[head * tokens : (head + 1) * tokens], out)
    return out


def softmax_parts(queries, keys, values, bias, heads, scale):
    scores = lax.dot_general(
        queries * jnp.asarray(scale, queries.dtype),
        keys,
        (((1,), (1,)), ((), ())),
        preferred_element_type=jnp.float32,
    )
    scores = scores + bias
    top = jnp.max(scores, axis=1, keepdims=True)
    exponent = jnp.exp(scores - top)
    total = jnp.sum(exponent, axis=1, keepdims=True)
    out = jnp.dot(exponent.astype(jnp.bfloat16), values, preferred_element_type=jnp.float32)
    return top, total, out


def put_stats(stats, first_head, heads, tokens, top, total):
    lane = lax.broadcasted_iota(jnp.int32, stats.shape, 1)
    for head in range(heads):
        rows = slice(head * tokens, (head + 1) * tokens)
        stats = jnp.where(lane == first_head + head, top[rows], stats)
        stats = jnp.where(lane == first_head + head + HD, total[rows], stats)
    return stats


def cache_kernel(scale, reqs, live, *refs):
    slots = reqs.shape[0]
    q_refs = refs[:slots]
    key_ref, value_ref, keep_ref, send_ref, key_out, value_out, key_buf, value_buf, in_sem, out_sem = refs[
        slots:
    ]
    tokens, width = q_refs[0].shape
    block_len = key_ref.shape[1]
    group = min(256, width)
    heads = group // HD
    sources, buffers, targets = (key_ref, value_ref), (key_buf, value_buf), (key_out, value_out)

    def fetch(slot, which):
        return pltpu.make_async_copy(
            sources[which].at[reqs[slot]], buffers[which].at[slot], in_sem.at[slot, which]
        )

    def store(slot, which):
        return pltpu.make_async_copy(
            buffers[which].at[slot], targets[which].at[reqs[slot]], out_sem.at[slot, which]
        )

    order = list(reversed(range(slots)))
    for slot in order:
        for which in range(2):
            fetch(slot, which).start()
    half = slots // 2
    for slot in order:
        count = live[reqs[slot]]
        row = lax.broadcasted_iota(jnp.int32, (1, block_len), 1)
        bias = jnp.where(row < count, 0.0, masked_low)
        some = count > 0
        target = send_ref if slot >= half else keep_ref
        place = slot % half
        stats = jnp.zeros((tokens, LANES), jnp.float32)
        for start in range(0, width, group):
            columns = slice(start, start + group)
            queries = block_diagonal(q_refs[slot][:, columns], heads)
            if start == 0:
                fetch(slot, 0).wait()
            keys = key_buf[slot, :, columns]
            if start == 0:
                fetch(slot, 1).wait()
            top, total, out = softmax_parts(
                queries, keys, value_buf[slot, :, columns], bias, heads, scale
            )
            target[place, :, columns] = diagonal_blocks(out, heads, tokens)
            stats = put_stats(stats, start // HD, heads, tokens, top, total)
        target[place, :, width:] = stats
        for which in range(2):
            store(slot, which).start()
    for slot in order:
        for which in range(2):
            store(slot, which).wait()


def cache_attention(queries, cache_key, cache_value, reqs, live, scale):
    slots = len(queries)
    tokens, width = queries[0].shape
    block_len = cache_key.shape[1]
    vmem = pl.BlockSpec(memory_space=pltpu.VMEM)
    smem = pl.BlockSpec(memory_space=pltpu.SMEM)
    hbm = pl.BlockSpec(memory_space=pltpu.HBM)
    part = jax.ShapeDtypeStruct((slots // 2, tokens, width + LANES), jnp.float32)
    cache = jax.ShapeDtypeStruct(cache_key.shape, cache_key.dtype)
    return pl.pallas_call(
        functools.partial(cache_kernel, scale),
        in_specs=[smem, smem] + [vmem] * slots + [hbm, hbm],
        out_specs=[vmem, vmem, hbm, hbm],
        out_shape=[part, part, cache, cache],
        scratch_shapes=[
            pltpu.VMEM(cache_key.shape, cache_key.dtype),
            pltpu.VMEM(cache_key.shape, cache_key.dtype),
            pltpu.SemaphoreType.DMA((slots, 2)),
            pltpu.SemaphoreType.DMA((slots, 2)),
        ],
        compiler_params=pltpu.CompilerParams(vmem_limit_bytes=40 * 1024 * 1024),
        cost_estimate=pl.CostEstimate(
            flops=16 * slots * tokens * width * block_len,
            transcendentals=slots * tokens * (width // HD) * block_len,
            bytes_accessed=8 * slots * block_len * width,
        ),
        name="cache_attention",
    )(reqs, live, *queries, cache_key, cache_value)


def tree_kernel(scale, q_ref, kv_ref, tree_ref, out_ref):
    tokens, width = q_ref.shape
    group = min(256, width)
    heads = group // HD
    allowed = jnp.concatenate([tree_ref[...]] * heads, axis=0) > 0.5
    bias = jnp.where(allowed, 0.0, masked_low)
    stats = jnp.zeros((tokens, LANES), jnp.float32)
    for start in range(0, width, group):
        columns = slice(start, start + group)
        queries = block_diagonal(q_ref[:, columns], heads)
        values = kv_ref[:, width + start : width + start + group]
        top, total, out = softmax_parts(queries, kv_ref[:, columns], values, bias, heads, scale)
        out_ref[:, columns] = diagonal_blocks(out, heads, tokens)
        stats = put_stats(stats, start // HD, heads, tokens, top, total)
    out_ref[:, width:] = stats


def tree_attention(queries, key_value, tree, scale):
    tokens, width = queries.shape
    return pl.pallas_call(
        functools.partial(tree_kernel, scale),
        out_shape=jax.ShapeDtypeStruct((tokens, width + LANES), jnp.float32),
        cost_estimate=pl.CostEstimate(
            flops=16 * tokens * width * tokens, transcendentals=tokens * tokens, bytes_accessed=10**6
        ),
        name="tree_attention",
    )(queries, key_value, tree)


def merged(parts, width):
    heads = width // HD
    tops = [part[..., width : width + heads] for part in parts]
    totals = [part[..., width + HD : width + HD + heads] for part in parts]
    top = functools.reduce(jnp.maximum, tops)
    scales = [jnp.exp(one - top) for one in tops]
    total = sum(one * by for one, by in zip(totals, scales))

    def spread(value):
        wide = jnp.broadcast_to(value[..., None], value.shape + (HD,))
        return wide.reshape(value.shape[:-1] + (width,))

    out = sum(part[..., :width] * spread(by) for part, by in zip(parts, scales))
    return out, top, total, spread


def merge(one, two, width):
    out, top, total, _ = merged([one, two], width)
    gap = jnp.zeros(top.shape[:-1] + (HD - top.shape[-1],), jnp.float32)
    return jnp.concatenate([out, top, gap, total, gap], axis=-1)


def patch_kernel(rows, reqs, firsts, starts, sel_ref, *refs):
    slots = reqs.shape[0]
    kv_refs = refs[:slots]
    key_ref, value_ref, key_out, value_out, key_buf, value_buf, in_sem, out_sem = refs[slots:]
    tokens = sel_ref.shape[1]
    width = key_ref.shape[2]
    sources, buffers, targets = (key_ref, value_ref), (key_buf, value_buf), (key_out, value_out)

    def window(ref, slot):
        request = reqs[slot]
        return ref.at[request, pl.ds(pl.multiple_of(firsts[request], 16), rows)]

    def fetch(slot, which):
        return pltpu.make_async_copy(
            window(sources[which], slot), buffers[which].at[slot], in_sem.at[slot, which]
        )

    def store(slot, which):
        return pltpu.make_async_copy(
            buffers[which].at[slot], window(targets[which], slot), out_sem.at[slot, which]
        )

    for slot in range(slots):
        for which in range(2):
            fetch(slot, which).start()
    for slot in range(slots):
        request = reqs[slot]
        offset = firsts[request] - starts[request]
        row = lax.broadcasted_iota(jnp.int32, (rows, tokens), 0) + offset
        depth = lax.broadcasted_iota(jnp.int32, (rows, tokens), 1)
        hits = jnp.where(row == depth, 1.0, 0.0).astype(jnp.bfloat16)
        picks = jnp.dot(hits, sel_ref[request], preferred_element_type=jnp.float32)
        touched = jnp.sum(picks, axis=1, keepdims=True) > 0.5
        picks = picks.astype(jnp.bfloat16)
        for which in range(2):
            fresh = kv_refs[slot][:, which * width : (which + 1) * width]
            written = jnp.dot(picks, fresh, preferred_element_type=jnp.float32)
            fetch(slot, which).wait()
            buffer = buffers[which]
            buffer[slot] = jnp.where(touched, written.astype(jnp.bfloat16), buffer[slot])
            store(slot, which).start()
    for slot in range(slots):
        for which in range(2):
            store(slot, which).wait()


def patch(key_values, reqs, selector, starts, keys, values):
    requests, block_len, width = keys.shape
    tokens = selector.shape[1]
    rows = tokens + 16
    firsts = jnp.clip(starts // 16 * 16, 0, block_len - rows)
    vmem = pl.BlockSpec(memory_space=pltpu.VMEM)
    smem = pl.BlockSpec(memory_space=pltpu.SMEM)
    hbm = pl.BlockSpec(memory_space=pltpu.HBM)
    return pl.pallas_call(
        functools.partial(patch_kernel, rows),
        in_specs=[smem] * 3 + [vmem] * (1 + requests) + [hbm] * 2,
        out_specs=[hbm, hbm],
        out_shape=[jax.ShapeDtypeStruct(keys.shape, keys.dtype)] * 2,
        scratch_shapes=[
            pltpu.VMEM((requests, rows, width), keys.dtype),
            pltpu.VMEM((requests, rows, width), keys.dtype),
            pltpu.SemaphoreType.DMA((requests, 2)),
            pltpu.SemaphoreType.DMA((requests, 2)),
        ],
        input_output_aliases={4 + requests: 0, 5 + requests: 1},
        compiler_params=pltpu.CompilerParams(vmem_limit_bytes=8 * 1024 * 1024),
        cost_estimate=pl.CostEstimate(
            flops=0, transcendentals=0, bytes_accessed=8 * requests * rows * width
        ),
        name="patch",
    )(reqs, firsts, starts, selector, *key_values, keys, values)


def on_device(
    hidden,
    w_query,
    w_key,
    w_value,
    w_out,
    cache_key,
    cache_value,
    parents,
    lengths,
    holder,
    selector,
):
    requests, tree_size = parents.shape
    width = w_query.shape[1]
    block_len = cache_key.shape[1]
    block_count = holder.shape[1]
    scale = 1.0 / math.sqrt(HD)
    axis = "blocks"
    index = lax.axis_index(axis)
    levels = requests.bit_length() - 1
    bits = block_count.bit_length() - 1
    assert 1 << levels == requests and 1 << bits == block_count and bits > levels
    split = [1 << s for s in range(levels)]
    whole = [1 << s for s in range(levels, bits)]
    own = sum(((index >> s) & 1) << (levels - 1 - s) for s in range(levels))
    reqs = own ^ jnp.arange(requests, dtype=jnp.int32)

    slots = jnp.arange(block_count, dtype=jnp.int32)
    logical = jnp.sum(slots[None, :] * (holder == index).astype(jnp.int32), axis=1)
    starts = lengths - logical * block_len
    live = jnp.clip(starts, 0, block_len)

    blocks_of = hidden.reshape(requests, tree_size, -1)
    rows = [lax.dynamic_index_in_dim(blocks_of, reqs[k], 0, False) for k in range(requests)]
    half = requests // 2
    send_rows = jnp.concatenate(rows[half:], axis=0)
    keep_rows = jnp.concatenate(rows[:half], axis=0)

    def scattered(weights):
        sent = jnp.dot(send_rows, weights, preferred_element_type=jnp.float32)
        sent = swap(sent, axis, split[0])
        value = jnp.dot(keep_rows, weights, preferred_element_type=jnp.float32) + sent
        for bit in split[1:]:
            middle = value.shape[0] // 2
            value = value[:middle] + swap(value[middle:], axis, bit)
        return value

    def reduced(value):
        for bit in whole:
            value = value + swap(value, axis, bit)
        return value

    def gathered(value):
        values = [value]
        for bit in reversed(split):
            values = values + [swap(one, axis, bit) for one in values]
        return values

    query_part = scattered(w_query)
    late_parents, late_lengths = lax.optimization_barrier((parents, lengths))
    ancestors = ancestry(lax.dynamic_index_in_dim(late_parents, own, 0, False))
    depths = (jnp.sum(ancestors, axis=1) - 1.0).astype(jnp.int32)
    positions = lax.dynamic_index_in_dim(late_lengths, own, 0, False) + depths
    tables = rotary_tables(positions)

    query_own = rotate(reduced(query_part), tables).astype(jnp.bfloat16)
    key_value = reduced(scattered(jnp.concatenate([w_key, w_value], axis=1)))
    kv_own = jnp.concatenate([rotate(key_value[:, :width], tables), key_value[:, width:]], axis=1)
    kv_own = kv_own.astype(jnp.bfloat16)

    queries = gathered(query_own)
    keep, send, keys_copied, values_copied = cache_attention(
        queries, cache_key, cache_value, reqs, live, scale
    )
    cached = merge(keep, swap(send, axis, split[0]), width)
    for bit in split[1:]:
        middle = cached.shape[0] // 2
        cached = merge(cached[:middle], swap(cached[middle:], axis, bit), width)
    cached = cached[0]
    for bit in whole[:-1]:
        cached = merge(cached, swap(cached, axis, bit), width)
    tree = tree_attention(query_own, kv_own, ancestors, scale)
    out, _, total, spread = merged([cached, swap(cached, axis, whole[-1]), tree], width)
    attended_own = (out / spread(total)).astype(jnp.bfloat16)

    mixed = [
        jnp.dot(one, w_out, preferred_element_type=jnp.float32) for one in gathered(attended_own)
    ]
    natural = []
    for request in range(requests):
        row = mixed[0]
        for k in range(1, requests):
            row = jnp.where(own == request ^ k, mixed[k], row)
        natural.append(row)
    mixed = jnp.concatenate(natural, axis=0)
    head_bit = lax.axis_size("heads") // 2
    while head_bit:
        high = (lax.axis_index("heads") & head_bit) > 0
        middle = mixed.shape[0] // 2
        kept = jnp.where(high, mixed[middle:], mixed[:middle])
        sent = jnp.where(high, mixed[:middle], mixed[middle:])
        mixed = kept + swap(sent, "heads", head_bit)
        head_bit //= 2
    mixed = mixed.astype(jnp.bfloat16)

    key_out, value_out = patch(
        gathered(kv_own), reqs, selector.astype(jnp.bfloat16), starts, keys_copied, values_copied
    )
    return (mixed, key_out, value_out)


def solution(mesh):
    return jax.shard_map(
        on_device,
        mesh=mesh,
        in_specs=(
            P(None, "blocks"),
            P("blocks", "heads"),
            P("blocks", "heads"),
            P("blocks", "heads"),
            P("heads", "blocks"),
            P(None, "blocks", "heads"),
            P(None, "blocks", "heads"),
            P(),
            P(),
            P(),
            P(),
        ),
        out_specs=(P("heads", "blocks"), P(None, "blocks", "heads"), P(None, "blocks", "heads")),
        check_vma=False,
    )
```

```python
import functools
import math

import jax
import jax.numpy as jnp
from jax import lax
from jax.experimental import pallas as pl
from jax.experimental.pallas import tpu as pltpu
from jax.sharding import PartitionSpec as P

HD = 64
ROT = 32
LANES = 128


masked_low = -1e30
rotary_base = 10000.0


def swap(value, axis, bit):
    size = lax.axis_size(axis)
    return lax.ppermute(value, axis, [(i, i ^ bit) for i in range(size)])


def ancestry(parents):
    tree_size = parents.shape[0]
    nodes = jnp.arange(tree_size, dtype=jnp.int32)
    parent_hop = ((parents[:, None] == nodes[None, :]) & (nodes[:, None] > 0)).astype(jnp.float32)
    reached = jnp.eye(tree_size, dtype=jnp.float32) + parent_hop
    for _ in range(tree_size.bit_length()):
        reached = jnp.minimum(jnp.dot(reached, reached, precision=lax.Precision.HIGHEST), 1.0)
    return reached


def rotary_tables(positions):
    column = jnp.arange(LANES, dtype=jnp.int32) % HD
    half = ROT // 2
    exponent = (column % half).astype(jnp.float32)
    inverse_freq = rotary_base ** (-2.0 * exponent / ROT)
    angles = positions.astype(jnp.float32)[:, None] * inverse_freq[None, :]
    cosine = jnp.where(column < ROT, jnp.cos(angles), 1.0)
    sine = jnp.sin(angles)
    ahead = jnp.where(column < half, -sine, 0.0)
    behind = jnp.where((column >= half) & (column < ROT), sine, 0.0)
    return jnp.stack([cosine, ahead, behind])


def rotate(value, tables):
    half = ROT // 2
    tables = jnp.tile(tables, (1, 1, value.shape[1] // LANES))
    ahead = jnp.roll(value, -half, axis=1)
    behind = jnp.roll(value, half, axis=1)
    return value * tables[0] + ahead * tables[1] + behind * tables[2]


def block_diagonal(queries, heads):
    tokens, width = queries.shape
    tall = jnp.concatenate([queries] * heads, axis=0)
    shape = (heads * tokens, width)
    row_head = lax.broadcasted_iota(jnp.int32, shape, 0) // tokens
    column_head = lax.broadcasted_iota(jnp.int32, shape, 1) // HD
    return jnp.where(row_head == column_head, tall, jnp.zeros_like(tall))


def diagonal_blocks(tall, heads, tokens):
    width = tall.shape[1]
    column_head = lax.broadcasted_iota(jnp.int32, (tokens, width), 1) // HD
    out = tall[:tokens]
    for head in range(1, heads):
        out = jnp.where(column_head == head, tall[head * tokens : (head + 1) * tokens], out)
    return out


def softmax_parts(queries, keys, values, bias, heads, scale):
    scores = lax.dot_general(
        queries * jnp.asarray(scale, queries.dtype),
        keys,
        (((1,), (1,)), ((), ())),
        preferred_element_type=jnp.float32,
    )
    scores = scores + bias
    top = jnp.max(scores, axis=1, keepdims=True)
    exponent = jnp.exp(scores - top)
    total = jnp.sum(exponent, axis=1, keepdims=True)
    out = jnp.dot(exponent.astype(jnp.bfloat16), values, preferred_element_type=jnp.float32)
    return top, total, out


def put_stats(stats, first_head, heads, tokens, top, total):
    lane = lax.broadcasted_iota(jnp.int32, stats.shape, 1)
    for head in range(heads):
        rows = slice(head * tokens, (head + 1) * tokens)
        stats = jnp.where(lane == first_head + head, top[rows], stats)
        stats = jnp.where(lane == first_head + head + HD, total[rows], stats)
    return stats


def cache_kernel(scale, reqs, live, *refs):
    slots = reqs.shape[0]
    q_refs = refs[:slots]
    key_ref, value_ref, keep_ref, send_ref, key_out, value_out, key_buf, value_buf, in_sem, out_sem = refs[
        slots:
    ]
    tokens, width = q_refs[0].shape
    block_len = key_ref.shape[1]
    group = min(256, width)
    heads = group // HD
    sources, buffers, targets = (key_ref, value_ref), (key_buf, value_buf), (key_out, value_out)

    def fetch(slot, which):
        return pltpu.make_async_copy(
            sources[which].at[reqs[slot]], buffers[which].at[slot], in_sem.at[slot, which]
        )

    def store(slot, which):
        return pltpu.make_async_copy(
            buffers[which].at[slot], targets[which].at[reqs[slot]], out_sem.at[slot, which]
        )

    order = list(reversed(range(slots)))
    for slot in order:
        for which in range(2):
            fetch(slot, which).start()
    half = slots // 2
    for slot in order:
        count = live[reqs[slot]]
        row = lax.broadcasted_iota(jnp.int32, (1, block_len), 1)
        bias = jnp.where(row < count, 0.0, masked_low)
        target = send_ref if slot >= half else keep_ref
        place = slot % half
        stats = jnp.zeros((tokens, LANES), jnp.float32)
        for start in range(0, width, group):
            columns = slice(start, start + group)
            queries = block_diagonal(q_refs[slot][:, columns], heads)
            if start == 0:
                fetch(slot, 0).wait()
            keys = key_buf[slot, :, columns]
            if start == 0:
                fetch(slot, 1).wait()
            top, total, out = softmax_parts(
                queries, keys, value_buf[slot, :, columns], bias, heads, scale
            )
            target[place, :, columns] = diagonal_blocks(out, heads, tokens)
            stats = put_stats(stats, start // HD, heads, tokens, top, total)
        target[place, :, width:] = stats
        for which in range(2):
            store(slot, which).start()
    for slot in order:
        for which in range(2):
            store(slot, which).wait()


def cache_attention(queries, cache_key, cache_value, reqs, live, scale):
    slots = len(queries)
    tokens, width = queries[0].shape
    block_len = cache_key.shape[1]
    vmem = pl.BlockSpec(memory_space=pltpu.VMEM)
    smem = pl.BlockSpec(memory_space=pltpu.SMEM)
    hbm = pl.BlockSpec(memory_space=pltpu.HBM)
    part = jax.ShapeDtypeStruct((slots // 2, tokens, width + LANES), jnp.float32)
    cache = jax.ShapeDtypeStruct(cache_key.shape, cache_key.dtype)
    return pl.pallas_call(
        functools.partial(cache_kernel, scale),
        in_specs=[smem, smem] + [vmem] * slots + [hbm, hbm],
        out_specs=[vmem, vmem, hbm, hbm],
        out_shape=[part, part, cache, cache],
        scratch_shapes=[
            pltpu.VMEM(cache_key.shape, cache_key.dtype),
            pltpu.VMEM(cache_key.shape, cache_key.dtype),
            pltpu.SemaphoreType.DMA((slots, 2)),
            pltpu.SemaphoreType.DMA((slots, 2)),
        ],
        compiler_params=pltpu.CompilerParams(vmem_limit_bytes=58 * 1024 * 1024),
        cost_estimate=pl.CostEstimate(
            flops=16 * slots * tokens * width * block_len,
            transcendentals=slots * tokens * (width // HD) * block_len,
            bytes_accessed=8 * slots * block_len * width,
        ),
        name="cache_attention",
    )(reqs, live, *queries, cache_key, cache_value)


def tree_kernel(scale, q_ref, kv_ref, tree_ref, out_ref):
    tokens, width = q_ref.shape
    group = min(256, width)
    heads = group // HD
    allowed = jnp.concatenate([tree_ref[...]] * heads, axis=0) > 0.5
    bias = jnp.where(allowed, 0.0, masked_low)
    stats = jnp.zeros((tokens, LANES), jnp.float32)
    for start in range(0, width, group):
        columns = slice(start, start + group)
        queries = block_diagonal(q_ref[:, columns], heads)
        values = kv_ref[:, width + start : width + start + group]
        top, total, out = softmax_parts(queries, kv_ref[:, columns], values, bias, heads, scale)
        out_ref[:, columns] = diagonal_blocks(out, heads, tokens)
        stats = put_stats(stats, start // HD, heads, tokens, top, total)
    out_ref[:, width:] = stats


def tree_attention(queries, key_value, tree, scale):
    tokens, width = queries.shape
    return pl.pallas_call(
        functools.partial(tree_kernel, scale),
        out_shape=jax.ShapeDtypeStruct((tokens, width + LANES), jnp.float32),
        cost_estimate=pl.CostEstimate(
            flops=16 * tokens * width * tokens, transcendentals=tokens * tokens, bytes_accessed=10**6
        ),
        name="tree_attention",
    )(queries, key_value, tree)


def spread(value, width):
    wide = jnp.broadcast_to(value[..., None], value.shape + (HD,))
    return wide.reshape(value.shape[:-1] + (width,))


def merged_stats(parts, width):
    heads = width // HD
    tops = [part[..., width : width + heads] for part in parts]
    totals = [part[..., width + HD : width + HD + heads] for part in parts]
    top = functools.reduce(jnp.maximum, tops)
    scales = [jnp.exp(one - top) for one in tops]
    total = sum(one * by for one, by in zip(totals, scales))
    return scales, top, total


def merge(one, two, width):
    scales, top, total = merged_stats([one, two], width)
    out = sum(part[..., :width] * spread(by, width) for part, by in zip([one, two], scales))
    gap = jnp.zeros(top.shape[:-1] + (HD - top.shape[-1],), jnp.float32)
    return jnp.concatenate([out, top, gap, total, gap], axis=-1)


def blended(parts, width):
    scales, _, total = merged_stats(parts, width)
    return sum(part[..., :width] * spread(by / total, width) for part, by in zip(parts, scales))


def patch_kernel(rows, reqs, firsts, starts, sel_ref, *refs):
    slots = reqs.shape[0]
    kv_refs = refs[:slots]
    key_ref, value_ref, key_out, value_out, key_buf, value_buf, in_sem, out_sem = refs[slots:]
    tokens = sel_ref.shape[1]
    width = key_ref.shape[2]
    sources, buffers, targets = (key_ref, value_ref), (key_buf, value_buf), (key_out, value_out)

    def window(ref, slot):
        request = reqs[slot]
        return ref.at[request, pl.ds(pl.multiple_of(firsts[request], 16), rows)]

    def fetch(slot, which):
        return pltpu.make_async_copy(
            window(sources[which], slot), buffers[which].at[slot], in_sem.at[slot, which]
        )

    def store(slot, which):
        return pltpu.make_async_copy(
            buffers[which].at[slot], window(targets[which], slot), out_sem.at[slot, which]
        )

    for slot in range(slots):
        for which in range(2):
            fetch(slot, which).start()
    for slot in range(slots):
        request = reqs[slot]
        offset = firsts[request] - starts[request]
        row = lax.broadcasted_iota(jnp.int32, (rows, tokens), 0) + offset
        depth = lax.broadcasted_iota(jnp.int32, (rows, tokens), 1)
        hits = jnp.where(row == depth, 1.0, 0.0).astype(jnp.bfloat16)
        picks = jnp.dot(hits, sel_ref[request], preferred_element_type=jnp.float32)
        touched = jnp.sum(picks, axis=1, keepdims=True) > 0.5
        picks = picks.astype(jnp.bfloat16)
        for which in range(2):
            fresh = kv_refs[slot][:, which * width : (which + 1) * width]
            written = jnp.dot(picks, fresh, preferred_element_type=jnp.float32)
            fetch(slot, which).wait()
            buffer = buffers[which]
            buffer[slot] = jnp.where(touched, written.astype(jnp.bfloat16), buffer[slot])
            store(slot, which).start()
    for slot in range(slots):
        for which in range(2):
            store(slot, which).wait()


def patch(key_values, reqs, selector, starts, keys, values):
    requests, block_len, width = keys.shape
    tokens = selector.shape[1]
    rows = tokens + 16
    firsts = jnp.clip(starts // 16 * 16, 0, block_len - rows)
    vmem = pl.BlockSpec(memory_space=pltpu.VMEM)
    smem = pl.BlockSpec(memory_space=pltpu.SMEM)
    hbm = pl.BlockSpec(memory_space=pltpu.HBM)
    return pl.pallas_call(
        functools.partial(patch_kernel, rows),
        in_specs=[smem] * 3 + [vmem] * (1 + requests) + [hbm] * 2,
        out_specs=[hbm, hbm],
        out_shape=[jax.ShapeDtypeStruct(keys.shape, keys.dtype)] * 2,
        scratch_shapes=[
            pltpu.VMEM((requests, rows, width), keys.dtype),
            pltpu.VMEM((requests, rows, width), keys.dtype),
            pltpu.SemaphoreType.DMA((requests, 2)),
            pltpu.SemaphoreType.DMA((requests, 2)),
        ],
        input_output_aliases={4 + requests: 0, 5 + requests: 1},
        compiler_params=pltpu.CompilerParams(vmem_limit_bytes=8 * 1024 * 1024),
        cost_estimate=pl.CostEstimate(
            flops=0, transcendentals=0, bytes_accessed=8 * requests * rows * width
        ),
        name="patch",
    )(reqs, firsts, starts, selector, *key_values, keys, values)


def on_device(
    hidden,
    w_query,
    w_key,
    w_value,
    w_out,
    cache_key,
    cache_value,
    parents,
    lengths,
    holder,
    selector,
):
    requests, tree_size = parents.shape
    width = w_query.shape[1]
    block_len = cache_key.shape[1]
    block_count = holder.shape[1]
    scale = 1.0 / math.sqrt(HD)
    axis = "blocks"
    index = lax.axis_index(axis)
    levels = requests.bit_length() - 1
    bits = block_count.bit_length() - 1
    assert 1 << levels == requests and 1 << bits == block_count and bits > levels
    split = [1 << s for s in range(levels)]
    whole = [1 << s for s in range(levels, bits)]
    own = sum(((index >> s) & 1) << (levels - 1 - s) for s in range(levels))
    own = own.astype(jnp.int32)
    reqs = own ^ jnp.arange(requests, dtype=jnp.int32)

    slots = jnp.arange(block_count, dtype=jnp.int32)
    logical = jnp.sum(slots[None, :] * (holder == index).astype(jnp.int32), axis=1)
    starts = lengths - logical * block_len
    live = jnp.clip(starts, 0, block_len)

    def scattered(value):
        for bit in split[1:]:
            middle = value.shape[0] // 2
            value = value[:middle] + swap(value[middle:], axis, bit)
        return value

    def gathered(value):
        values = [value]
        for bit in reversed(split):
            values = values + [swap(one, axis, bit) for one in values]
        return values

    def tied(value, *others):
        return lax.optimization_barrier((value,) + others)

    def after(value, *others):
        return tied(value, *others)[0]

    half = requests // 2 * tree_size
    blocks_of = hidden.reshape(requests, tree_size, -1)
    rows = [lax.dynamic_index_in_dim(blocks_of, own ^ k, 0, False) for k in range(requests)]
    rows = jnp.concatenate(rows, axis=0)

    def first_sum(rows, weights):
        parts = [jnp.dot(rows, w, preferred_element_type=jnp.float32) for w in weights]
        sent = swap(jnp.concatenate([part[half:] for part in parts], axis=1), axis, split[0])
        return jnp.concatenate([part[:half] for part in parts], axis=1) + sent

    query_half = first_sum(rows, [w_query])
    kv_half = first_sum(after(rows, query_half), [w_key, w_value])
    query_sum = scattered(query_half)
    kv_half = after(kv_half, query_sum)
    late_parents, _ = tied(parents, query_sum)
    ancestors = ancestry(lax.dynamic_index_in_dim(late_parents, own, 0, False))
    query_sum = query_sum + swap(query_sum, axis, whole[0])
    query_sum, kv_half, ancestors = tied(query_sum, kv_half, ancestors)
    late_lengths, late_ancestors, _ = tied(lengths, ancestors, query_sum)
    depths = (jnp.sum(late_ancestors, axis=1) - 1.0).astype(jnp.int32)
    positions = lax.dynamic_index_in_dim(late_lengths, own, 0, False) + depths
    tables = rotary_tables(positions)

    kv_sum = scattered(kv_half)
    for bit in whole[1:]:
        query_sum = query_sum + swap(query_sum, axis, bit)
    query_own = rotate(query_sum, tables).astype(jnp.bfloat16)
    queries = gathered(query_own)
    takes_value = (index & whole[0]) > 0
    key_part, value_part = kv_sum[:, :width], kv_sum[:, width:]
    part = jnp.where(takes_value, value_part, key_part)
    part = part + swap(jnp.where(takes_value, key_part, value_part), axis, whole[0])
    *queries, part = tied(*queries, part)

    keep, send, keys_copied, values_copied = cache_attention(
        queries, cache_key, cache_value, reqs, live, scale
    )
    for bit in whole[1:]:
        part = part + swap(part, axis, bit)
    keep, send, part = tied(keep, send, part)
    part = jnp.where(takes_value, part, rotate(part, tables)).astype(jnp.bfloat16)
    far = swap(part, axis, whole[0])
    kv_own = jnp.concatenate(
        [jnp.where(takes_value, far, part), jnp.where(takes_value, part, far)], axis=1
    )
    cached = merge(keep, swap(send, axis, split[0]), width)
    for bit in split[1:]:
        middle = cached.shape[0] // 2
        cached = merge(cached[:middle], swap(cached[middle:], axis, bit), width)
    cached = cached[0]
    for bit in whole[:-1]:
        cached = merge(cached, swap(cached, axis, bit), width)
    tree = tree_attention(query_own, kv_own, ancestors, scale)
    key_out, value_out = patch(
        gathered(kv_own), reqs, selector.astype(jnp.bfloat16), starts, keys_copied, values_copied
    )
    other = swap(cached, axis, whole[-1])
    other, tree = tied(other, tree)
    attended_own = blended([cached, other, tree], width).astype(jnp.bfloat16)
    everyone = gathered(attended_own)
    everyone[1], key_out, value_out = tied(everyone[1], key_out, value_out)

    mixed = [jnp.dot(one, w_out, preferred_element_type=jnp.float32) for one in everyone]
    natural = []
    for request in range(requests):
        row = mixed[0]
        for k in range(1, requests):
            row = jnp.where(own == request ^ k, mixed[k], row)
        natural.append(row)
    mixed = jnp.concatenate(natural, axis=0)
    head_bit = lax.axis_size("heads") // 2
    while head_bit:
        high = (lax.axis_index("heads") & head_bit) > 0
        middle = mixed.shape[0] // 2
        kept = jnp.where(high, mixed[middle:], mixed[:middle])
        sent = jnp.where(high, mixed[:middle], mixed[middle:])
        mixed = kept + swap(sent, "heads", head_bit)
        head_bit //= 2
    mixed = mixed.astype(jnp.bfloat16)

    return (mixed, key_out, value_out)


def solution(mesh):
    return jax.shard_map(
        on_device,
        mesh=mesh,
        in_specs=(
            P(None, "blocks"),
            P("blocks", "heads"),
            P("blocks", "heads"),
            P("blocks", "heads"),
            P("heads", "blocks"),
            P(None, "blocks", "heads"),
            P(None, "blocks", "heads"),
            P(),
            P(),
            P(),
            P(),
        ),
        out_specs=(P("heads", "blocks"), P(None, "blocks", "heads"), P(None, "blocks", "heads")),
        check_vma=False,
    )
```

```python
import functools
import math

import jax
import jax.numpy as jnp
from jax import lax
from jax.experimental import pallas as pl
from jax.experimental.pallas import tpu as pltpu
from jax.sharding import PartitionSpec as P

HD = 64
ROT = 32
LANES = 128


masked_low = -1e30
rotary_base = 10000.0


def swap(value, axis, bit):
    size = lax.axis_size(axis)
    return lax.ppermute(value, axis, [(i, i ^ bit) for i in range(size)])


def ancestry(parents):
    tree_size = parents.shape[0]
    nodes = jnp.arange(tree_size, dtype=jnp.int32)
    parent_hop = ((parents[:, None] == nodes[None, :]) & (nodes[:, None] > 0)).astype(jnp.float32)
    reached = jnp.eye(tree_size, dtype=jnp.float32) + parent_hop
    for _ in range(tree_size.bit_length()):
        reached = jnp.minimum(jnp.dot(reached, reached, precision=lax.Precision.HIGHEST), 1.0)
    return reached


def rotary_tables(positions):
    column = jnp.arange(LANES, dtype=jnp.int32) % HD
    half = ROT // 2
    exponent = (column % half).astype(jnp.float32)
    inverse_freq = rotary_base ** (-2.0 * exponent / ROT)
    angles = positions.astype(jnp.float32)[:, None] * inverse_freq[None, :]
    cosine = jnp.where(column < ROT, jnp.cos(angles), 1.0)
    sine = jnp.sin(angles)
    ahead = jnp.where(column < half, -sine, 0.0)
    behind = jnp.where((column >= half) & (column < ROT), sine, 0.0)
    return jnp.stack([cosine, ahead, behind])


def rotate(value, tables):
    half = ROT // 2
    tables = jnp.tile(tables, (1, 1, value.shape[1] // LANES))
    ahead = jnp.roll(value, -half, axis=1)
    behind = jnp.roll(value, half, axis=1)
    return value * tables[0] + ahead * tables[1] + behind * tables[2]


def block_diagonal(queries, heads):
    tokens, width = queries.shape
    tall = jnp.concatenate([queries] * heads, axis=0)
    shape = (heads * tokens, width)
    row_head = lax.broadcasted_iota(jnp.int32, shape, 0) // tokens
    column_head = lax.broadcasted_iota(jnp.int32, shape, 1) // HD
    return jnp.where(row_head == column_head, tall, jnp.zeros_like(tall))


def diagonal_blocks(tall, heads, tokens):
    width = tall.shape[1]
    column_head = lax.broadcasted_iota(jnp.int32, (tokens, width), 1) // HD
    out = tall[:tokens]
    for head in range(1, heads):
        out = jnp.where(column_head == head, tall[head * tokens : (head + 1) * tokens], out)
    return out


def softmax_parts(queries, keys, values, bias, heads, scale):
    scores = lax.dot_general(
        queries * jnp.asarray(scale, queries.dtype),
        keys,
        (((1,), (1,)), ((), ())),
        preferred_element_type=jnp.float32,
    )
    scores = scores + bias
    top = jnp.max(scores, axis=1, keepdims=True)
    exponent = jnp.exp(scores - top)
    total = jnp.sum(exponent, axis=1, keepdims=True)
    out = jnp.dot(exponent.astype(jnp.bfloat16), values, preferred_element_type=jnp.float32)
    return top, total, out


def put_stats(stats, first_head, heads, tokens, top, total):
    lane = lax.broadcasted_iota(jnp.int32, stats.shape, 1)
    for head in range(heads):
        rows = slice(head * tokens, (head + 1) * tokens)
        stats = jnp.where(lane == first_head + head, top[rows], stats)
        stats = jnp.where(lane == first_head + head + HD, total[rows], stats)
    return stats


def cache_kernel(scale, reqs, live, *refs):
    slots = reqs.shape[0]
    q_refs = refs[:slots]
    key_ref, value_ref, keep_ref, send_ref, key_out, value_out, key_buf, value_buf, in_sem, out_sem = refs[
        slots:
    ]
    tokens, width = q_refs[0].shape
    block_len = key_ref.shape[1]
    group = min(256, width)
    heads = group // HD
    sources, buffers, targets = (key_ref, value_ref), (key_buf, value_buf), (key_out, value_out)

    def fetch(slot, which):
        return pltpu.make_async_copy(
            sources[which].at[reqs[slot]], buffers[which].at[slot], in_sem.at[slot, which]
        )

    def store(slot, which):
        return pltpu.make_async_copy(
            buffers[which].at[slot], targets[which].at[reqs[slot]], out_sem.at[slot, which]
        )

    order = list(reversed(range(slots)))
    for slot in order:
        for which in range(2):
            fetch(slot, which).start()
    half = slots // 2
    for slot in order:
        count = live[reqs[slot]]
        row = lax.broadcasted_iota(jnp.int32, (1, block_len), 1)
        bias = jnp.where(row < count, 0.0, masked_low)
        target = send_ref if slot >= half else keep_ref
        place = slot % half
        stats = jnp.zeros((tokens, LANES), jnp.float32)
        for start in range(0, width, group):
            columns = slice(start, start + group)
            queries = block_diagonal(q_refs[slot][:, columns], heads)
            if start == 0:
                fetch(slot, 0).wait()
            keys = key_buf[slot, :, columns]
            if start == 0:
                fetch(slot, 1).wait()
            top, total, out = softmax_parts(
                queries, keys, value_buf[slot, :, columns], bias, heads, scale
            )
            target[place, :, columns] = diagonal_blocks(out, heads, tokens)
            stats = put_stats(stats, start // HD, heads, tokens, top, total)
        target[place, :, width:] = stats
        for which in range(2):
            store(slot, which).start()
    for slot in order:
        for which in range(2):
            store(slot, which).wait()


def cache_attention(queries, cache_key, cache_value, reqs, live, scale):
    slots = len(queries)
    tokens, width = queries[0].shape
    block_len = cache_key.shape[1]
    vmem = pl.BlockSpec(memory_space=pltpu.VMEM)
    smem = pl.BlockSpec(memory_space=pltpu.SMEM)
    hbm = pl.BlockSpec(memory_space=pltpu.HBM)
    part = jax.ShapeDtypeStruct((slots // 2, tokens, width + LANES), jnp.float32)
    cache = jax.ShapeDtypeStruct(cache_key.shape, cache_key.dtype)
    return pl.pallas_call(
        functools.partial(cache_kernel, scale),
        in_specs=[smem, smem] + [vmem] * slots + [hbm, hbm],
        out_specs=[vmem, vmem, hbm, hbm],
        out_shape=[part, part, cache, cache],
        scratch_shapes=[
            pltpu.VMEM(cache_key.shape, cache_key.dtype),
            pltpu.VMEM(cache_key.shape, cache_key.dtype),
            pltpu.SemaphoreType.DMA((slots, 2)),
            pltpu.SemaphoreType.DMA((slots, 2)),
        ],
        compiler_params=pltpu.CompilerParams(vmem_limit_bytes=48 * 1024 * 1024),
        cost_estimate=pl.CostEstimate(
            flops=16 * slots * tokens * width * block_len,
            transcendentals=slots * tokens * (width // HD) * block_len,
            bytes_accessed=8 * slots * block_len * width,
        ),
        name="cache_attention",
    )(reqs, live, *queries, cache_key, cache_value)


def tree_kernel(scale, q_ref, kv_ref, tree_ref, out_ref):
    tokens, width = q_ref.shape
    group = min(256, width)
    heads = group // HD
    allowed = jnp.concatenate([tree_ref[...]] * heads, axis=0) > 0.5
    bias = jnp.where(allowed, 0.0, masked_low)
    stats = jnp.zeros((tokens, LANES), jnp.float32)
    for start in range(0, width, group):
        columns = slice(start, start + group)
        queries = block_diagonal(q_ref[:, columns], heads)
        values = kv_ref[:, width + start : width + start + group]
        top, total, out = softmax_parts(queries, kv_ref[:, columns], values, bias, heads, scale)
        out_ref[:, columns] = diagonal_blocks(out, heads, tokens)
        stats = put_stats(stats, start // HD, heads, tokens, top, total)
    out_ref[:, width:] = stats


def tree_attention(queries, key_value, tree, scale):
    tokens, width = queries.shape
    return pl.pallas_call(
        functools.partial(tree_kernel, scale),
        out_shape=jax.ShapeDtypeStruct((tokens, width + LANES), jnp.float32),
        compiler_params=pltpu.CompilerParams(vmem_limit_bytes=8 * 1024 * 1024),
        cost_estimate=pl.CostEstimate(
            flops=16 * tokens * width * tokens, transcendentals=tokens * tokens, bytes_accessed=10**6
        ),
        name="tree_attention",
    )(queries, key_value, tree)


def spread(value, pair, shape):
    lane = lax.broadcasted_iota(jnp.int32, shape, 1)
    first = jnp.broadcast_to(value[:, 2 * pair : 2 * pair + 1], shape)
    second = jnp.broadcast_to(value[:, 2 * pair + 1 : 2 * pair + 2], shape)
    return jnp.where(lane < HD, first, second)


def merged_stats(stats):
    top = functools.reduce(jnp.maximum, stats)
    scales = [jnp.exp(one - top) for one in stats]
    total = sum(one * pltpu.roll(by, HD, axis=1) for one, by in zip(stats, scales))
    return scales, top, total


def merge_kernel(width, finish, *refs):
    *parts, out_ref = refs
    scales, top, total = merged_stats([part[:, width:] for part in parts])
    if finish:
        total = pltpu.roll(total, HD, axis=1)
        scales = [by / total for by in scales]
    else:
        lane = lax.broadcasted_iota(jnp.int32, top.shape, 1)
        out_ref[:, width:] = jnp.where(lane < HD, top, total)
    shape = (top.shape[0], LANES)
    for pair in range(width // LANES):
        columns = slice(pair * LANES, (pair + 1) * LANES)
        out = sum(part[:, columns] * spread(by, pair, shape) for part, by in zip(parts, scales))
        out_ref[:, columns] = out.astype(out_ref.dtype)


def merged(parts, width, finish):
    rows = parts[0].shape[0]
    if finish:
        shape = jax.ShapeDtypeStruct((rows, width), jnp.bfloat16)
    else:
        shape = jax.ShapeDtypeStruct((rows, width + LANES), jnp.float32)
    return pl.pallas_call(
        functools.partial(merge_kernel, width, finish),
        out_shape=shape,
        compiler_params=pltpu.CompilerParams(vmem_limit_bytes=4 * 1024 * 1024),
        cost_estimate=pl.CostEstimate(
            flops=4 * rows * width, transcendentals=rows * LANES, bytes_accessed=12 * rows * width
        ),
        name="merge",
    )(*parts)


def merge(one, two, width):
    return merged([one, two], width, False)


def patch_kernel(rows, reqs, firsts, starts, sel_ref, *refs):
    slots = reqs.shape[0]
    kv_refs = refs[:slots]
    key_ref, value_ref, key_out, value_out, key_buf, value_buf, in_sem, out_sem = refs[slots:]
    tokens = sel_ref.shape[1]
    width = key_ref.shape[2]
    sources, buffers, targets = (key_ref, value_ref), (key_buf, value_buf), (key_out, value_out)

    def window(ref, slot):
        request = reqs[slot]
        return ref.at[request, pl.ds(pl.multiple_of(firsts[request], 16), rows)]

    def fetch(slot, which):
        return pltpu.make_async_copy(
            window(sources[which], slot), buffers[which].at[slot], in_sem.at[slot, which]
        )

    def store(slot, which):
        return pltpu.make_async_copy(
            buffers[which].at[slot], window(targets[which], slot), out_sem.at[slot, which]
        )

    for slot in range(slots):
        for which in range(2):
            fetch(slot, which).start()
    for slot in range(slots):
        request = reqs[slot]
        offset = firsts[request] - starts[request]
        row = lax.broadcasted_iota(jnp.int32, (rows, tokens), 0) + offset
        depth = lax.broadcasted_iota(jnp.int32, (rows, tokens), 1)
        hits = jnp.where(row == depth, 1.0, 0.0).astype(jnp.bfloat16)
        picks = jnp.dot(hits, sel_ref[request], preferred_element_type=jnp.float32)
        touched = jnp.sum(picks, axis=1, keepdims=True) > 0.5
        picks = picks.astype(jnp.bfloat16)
        for which in range(2):
            fresh = kv_refs[slot][:, which * width : (which + 1) * width]
            written = jnp.dot(picks, fresh, preferred_element_type=jnp.float32)
            fetch(slot, which).wait()
            buffer = buffers[which]
            buffer[slot] = jnp.where(touched, written.astype(jnp.bfloat16), buffer[slot])
            store(slot, which).start()
    for slot in range(slots):
        for which in range(2):
            store(slot, which).wait()


def patch(key_values, reqs, selector, starts, keys, values):
    requests, block_len, width = keys.shape
    tokens = selector.shape[1]
    rows = tokens + 16
    firsts = jnp.clip(starts // 16 * 16, 0, block_len - rows)
    vmem = pl.BlockSpec(memory_space=pltpu.VMEM)
    smem = pl.BlockSpec(memory_space=pltpu.SMEM)
    hbm = pl.BlockSpec(memory_space=pltpu.HBM)
    return pl.pallas_call(
        functools.partial(patch_kernel, rows),
        in_specs=[smem] * 3 + [vmem] * (1 + requests) + [hbm] * 2,
        out_specs=[hbm, hbm],
        out_shape=[jax.ShapeDtypeStruct(keys.shape, keys.dtype)] * 2,
        scratch_shapes=[
            pltpu.VMEM((requests, rows, width), keys.dtype),
            pltpu.VMEM((requests, rows, width), keys.dtype),
            pltpu.SemaphoreType.DMA((requests, 2)),
            pltpu.SemaphoreType.DMA((requests, 2)),
        ],
        input_output_aliases={4 + requests: 0, 5 + requests: 1},
        compiler_params=pltpu.CompilerParams(vmem_limit_bytes=8 * 1024 * 1024),
        cost_estimate=pl.CostEstimate(
            flops=0, transcendentals=0, bytes_accessed=8 * requests * rows * width
        ),
        name="patch",
    )(reqs, firsts, starts, selector, *key_values, keys, values)


def on_device(
    hidden,
    w_query,
    w_key,
    w_value,
    w_out,
    cache_key,
    cache_value,
    parents,
    lengths,
    holder,
    selector,
):
    requests, tree_size = parents.shape
    width = w_query.shape[1]
    block_len = cache_key.shape[1]
    block_count = holder.shape[1]
    scale = 1.0 / math.sqrt(HD)
    axis = "blocks"
    index = lax.axis_index(axis)
    levels = requests.bit_length() - 1
    bits = block_count.bit_length() - 1
    assert 1 << levels == requests and 1 << bits == block_count and bits > levels
    split = [1 << s for s in range(levels)]
    whole = [1 << s for s in range(levels, bits)]
    own = sum(((index >> s) & 1) << (levels - 1 - s) for s in range(levels))
    own = own.astype(jnp.int32)
    reqs = own ^ jnp.arange(requests, dtype=jnp.int32)


    def scattered(value):
        for bit in split[1:]:
            middle = value.shape[0] // 2
            value = value[:middle] + swap(value[middle:], axis, bit)
        return value

    def gathered(value):
        values = [value]
        for bit in reversed(split):
            values = values + [swap(one, axis, bit) for one in values]
        return values

    def tied(value, *others):
        return lax.optimization_barrier((value,) + others)

    def after(value, *others):
        return tied(value, *others)[0]

    half = requests // 2 * tree_size
    blocks_of = hidden.reshape(requests, tree_size, -1)
    rows = [lax.dynamic_index_in_dim(blocks_of, own ^ k, 0, False) for k in range(requests)]
    rows = jnp.concatenate(rows, axis=0)

    def first_sum(rows, weights):
        parts = [jnp.dot(rows, w, preferred_element_type=jnp.float32) for w in weights]
        sent = swap(jnp.concatenate([part[half:] for part in parts], axis=1), axis, split[0])
        return jnp.concatenate([part[:half] for part in parts], axis=1) + sent

    query_half = first_sum(rows, [w_query])
    kv_half = first_sum(after(rows, query_half), [w_key, w_value])
    query_sum = scattered(query_half)
    kv_half = after(kv_half, query_sum)
    late_parents, _ = tied(parents, query_sum)
    ancestors = ancestry(lax.dynamic_index_in_dim(late_parents, own, 0, False))
    query_sum = query_sum + swap(query_sum, axis, whole[0])
    query_sum, kv_half, ancestors = tied(query_sum, kv_half, ancestors)
    late_holder = after(holder, query_sum)
    slots = jnp.arange(block_count, dtype=jnp.int32)
    logical = jnp.sum(slots[None, :] * (late_holder == index).astype(jnp.int32), axis=1)
    starts = lengths - logical * block_len
    live = jnp.clip(starts, 0, block_len)
    late_lengths, late_ancestors, _ = tied(lengths, ancestors, query_sum)
    depths = (jnp.sum(late_ancestors, axis=1) - 1.0).astype(jnp.int32)
    positions = lax.dynamic_index_in_dim(late_lengths, own, 0, False) + depths
    tables = rotary_tables(positions)

    kv_sum = scattered(kv_half)
    for bit in whole[1:]:
        query_sum = query_sum + swap(query_sum, axis, bit)
    query_own = rotate(query_sum, tables).astype(jnp.bfloat16)
    queries = gathered(query_own)
    takes_value = (index & whole[0]) > 0
    key_part, value_part = kv_sum[:, :width], kv_sum[:, width:]
    part = jnp.where(takes_value, value_part, key_part)
    part = part + swap(jnp.where(takes_value, key_part, value_part), axis, whole[0])
    *queries, part = tied(*queries, part)

    keep, send, keys_copied, values_copied = cache_attention(
        queries, cache_key, cache_value, reqs, live, scale
    )
    for bit in whole[1:]:
        part = part + swap(part, axis, bit)
    keep, send, part = tied(keep, send, part)
    part = jnp.where(takes_value, part, rotate(part, tables)).astype(jnp.bfloat16)
    far = swap(part, axis, whole[0])
    kv_own = jnp.concatenate(
        [jnp.where(takes_value, far, part), jnp.where(takes_value, part, far)], axis=1
    )
    keep = keep.reshape(-1, width + LANES)
    send = send.reshape(-1, width + LANES)
    cached = merge(keep, swap(send, axis, split[0]), width)
    for bit in split[1:]:
        middle = cached.shape[0] // 2
        cached = merge(cached[:middle], swap(cached[middle:], axis, bit), width)
    for bit in whole[:-1]:
        cached = merge(cached, swap(cached, axis, bit), width)
    tree = tree_attention(query_own, kv_own, ancestors, scale)
    key_out, value_out = patch(
        gathered(kv_own), reqs, selector.astype(jnp.bfloat16), starts, keys_copied, values_copied
    )
    other = swap(cached, axis, whole[-1])
    other, tree = tied(other, tree)
    attended_own = merged([cached, other, tree], width, True)
    everyone = gathered(attended_own)
    everyone[1], key_out, value_out = tied(everyone[1], key_out, value_out)

    mixed = [jnp.dot(one, w_out, preferred_element_type=jnp.float32) for one in everyone]
    natural = []
    for request in range(requests):
        row = mixed[0]
        for k in range(1, requests):
            row = jnp.where(own == request ^ k, mixed[k], row)
        natural.append(row)
    mixed = jnp.concatenate(natural, axis=0)
    head_bit = lax.axis_size("heads") // 2
    while head_bit:
        high = (lax.axis_index("heads") & head_bit) > 0
        middle = mixed.shape[0] // 2
        kept = jnp.where(high, mixed[middle:], mixed[:middle])
        sent = jnp.where(high, mixed[:middle], mixed[middle:])
        mixed = kept + swap(sent, "heads", head_bit)
        head_bit //= 2
    mixed = mixed.astype(jnp.bfloat16)

    return (mixed, key_out, value_out)


def solution(mesh):
    return jax.shard_map(
        on_device,
        mesh=mesh,
        in_specs=(
            P(None, "blocks"),
            P("blocks", "heads"),
            P("blocks", "heads"),
            P("blocks", "heads"),
            P("heads", "blocks"),
            P(None, "blocks", "heads"),
            P(None, "blocks", "heads"),
            P(),
            P(),
            P(),
            P(),
        ),
        out_specs=(P("heads", "blocks"), P(None, "blocks", "heads"), P(None, "blocks", "heads")),
        check_vma=False,
    )
```

```python
import functools
import math

import jax
import jax.numpy as jnp
from jax import lax
from jax.experimental import pallas as pl
from jax.experimental.pallas import tpu as pltpu
from jax.sharding import PartitionSpec as P

HD = 64
ROT = 32
LANES = 128


masked_low = -1e30
rotary_base = 10000.0


def swap(value, axis, bit):
    size = lax.axis_size(axis)
    return lax.ppermute(value, axis, [(i, i ^ bit) for i in range(size)])


def ancestry(parents):
    tree_size = parents.shape[0]
    nodes = jnp.arange(tree_size, dtype=jnp.int32)
    parent_hop = ((parents[:, None] == nodes[None, :]) & (nodes[:, None] > 0)).astype(jnp.float32)
    reached = jnp.eye(tree_size, dtype=jnp.float32) + parent_hop
    for _ in range(tree_size.bit_length()):
        reached = jnp.minimum(jnp.dot(reached, reached, precision=lax.Precision.HIGHEST), 1.0)
    return reached


def rotary_tables(positions):
    column = jnp.arange(LANES, dtype=jnp.int32) % HD
    half = ROT // 2
    exponent = (column % half).astype(jnp.float32)
    inverse_freq = rotary_base ** (-2.0 * exponent / ROT)
    angles = positions.astype(jnp.float32)[:, None] * inverse_freq[None, :]
    cosine = jnp.where(column < ROT, jnp.cos(angles), 1.0)
    sine = jnp.sin(angles)
    ahead = jnp.where(column < half, -sine, 0.0)
    behind = jnp.where((column >= half) & (column < ROT), sine, 0.0)
    return jnp.stack([cosine, ahead, behind])


def rotate(value, tables):
    half = ROT // 2
    tables = jnp.tile(tables, (1, 1, value.shape[1] // LANES))
    ahead = jnp.roll(value, -half, axis=1)
    behind = jnp.roll(value, half, axis=1)
    return value * tables[0] + ahead * tables[1] + behind * tables[2]


def block_diagonal(queries, heads):
    tokens, width = queries.shape
    tall = jnp.concatenate([queries] * heads, axis=0)
    shape = (heads * tokens, width)
    row_head = lax.broadcasted_iota(jnp.int32, shape, 0) // tokens
    column_head = lax.broadcasted_iota(jnp.int32, shape, 1) // HD
    return jnp.where(row_head == column_head, tall, jnp.zeros_like(tall))


def diagonal_blocks(tall, heads, tokens):
    width = tall.shape[1]
    column_head = lax.broadcasted_iota(jnp.int32, (tokens, width), 1) // HD
    out = tall[:tokens]
    for head in range(1, heads):
        out = jnp.where(column_head == head, tall[head * tokens : (head + 1) * tokens], out)
    return out


def softmax_parts(queries, keys, values, bias, heads, scale):
    scores = lax.dot_general(
        queries * jnp.asarray(scale, queries.dtype),
        keys,
        (((1,), (1,)), ((), ())),
        preferred_element_type=jnp.float32,
    )
    scores = scores + bias
    top = jnp.max(scores, axis=1, keepdims=True)
    exponent = jnp.exp(scores - top)
    total = jnp.sum(exponent, axis=1, keepdims=True)
    out = jnp.dot(exponent.astype(jnp.bfloat16), values, preferred_element_type=jnp.float32)
    return top, total, out


def put_stats(stats, first_head, heads, tokens, top, total):
    lane = lax.broadcasted_iota(jnp.int32, stats.shape, 1)
    for head in range(heads):
        rows = slice(head * tokens, (head + 1) * tokens)
        stats = jnp.where(lane == first_head + head, top[rows], stats)
        stats = jnp.where(lane == first_head + head + HD, total[rows], stats)
    return stats


def cache_kernel(scale, reqs, live, *refs):
    slots = reqs.shape[0]
    q_refs = refs[:slots]
    key_ref, value_ref, keep_ref, send_ref, key_out, value_out, key_buf, value_buf, in_sem, out_sem = refs[
        slots:
    ]
    tokens, width = q_refs[0].shape
    block_len = key_ref.shape[1]
    group = min(256, width)
    heads = group // HD
    sources, buffers, targets = (key_ref, value_ref), (key_buf, value_buf), (key_out, value_out)

    def fetch(slot, which):
        return pltpu.make_async_copy(
            sources[which].at[reqs[slot]], buffers[which].at[slot], in_sem.at[slot, which]
        )

    def store(slot, which):
        return pltpu.make_async_copy(
            buffers[which].at[slot], targets[which].at[reqs[slot]], out_sem.at[slot, which]
        )

    order = list(reversed(range(slots)))
    for slot in order:
        for which in range(2):
            fetch(slot, which).start()
    half = slots // 2
    for slot in order:
        count = live[reqs[slot]]
        row = lax.broadcasted_iota(jnp.int32, (1, block_len), 1)
        bias = jnp.where(row < count, 0.0, masked_low)
        target = send_ref if slot >= half else keep_ref
        place = slot % half
        stats = jnp.zeros((tokens, LANES), jnp.float32)
        for start in range(0, width, group):
            columns = slice(start, start + group)
            queries = block_diagonal(q_refs[slot][:, columns], heads)
            if start == 0:
                fetch(slot, 0).wait()
            keys = key_buf[slot, :, columns]
            if start == 0:
                fetch(slot, 1).wait()
            top, total, out = softmax_parts(
                queries, keys, value_buf[slot, :, columns], bias, heads, scale
            )
            target[place, :, columns] = diagonal_blocks(out, heads, tokens)
            stats = put_stats(stats, start // HD, heads, tokens, top, total)
        target[place, :, width:] = stats
        for which in range(2):
            store(slot, which).start()
    for slot in order:
        for which in range(2):
            store(slot, which).wait()


def cache_attention(queries, cache_key, cache_value, reqs, live, scale):
    slots = len(queries)
    tokens, width = queries[0].shape
    block_len = cache_key.shape[1]
    vmem = pl.BlockSpec(memory_space=pltpu.VMEM)
    smem = pl.BlockSpec(memory_space=pltpu.SMEM)
    hbm = pl.BlockSpec(memory_space=pltpu.HBM)
    part = jax.ShapeDtypeStruct((slots // 2, tokens, width + LANES), jnp.float32)
    cache = jax.ShapeDtypeStruct(cache_key.shape, cache_key.dtype)
    return pl.pallas_call(
        functools.partial(cache_kernel, scale),
        in_specs=[smem, smem] + [vmem] * slots + [hbm, hbm],
        out_specs=[vmem, vmem, hbm, hbm],
        out_shape=[part, part, cache, cache],
        scratch_shapes=[
            pltpu.VMEM(cache_key.shape, cache_key.dtype),
            pltpu.VMEM(cache_key.shape, cache_key.dtype),
            pltpu.SemaphoreType.DMA((slots, 2)),
            pltpu.SemaphoreType.DMA((slots, 2)),
        ],
        compiler_params=pltpu.CompilerParams(vmem_limit_bytes=48 * 1024 * 1024),
        cost_estimate=pl.CostEstimate(
            flops=16 * slots * tokens * width * block_len,
            transcendentals=slots * tokens * (width // HD) * block_len,
            bytes_accessed=8 * slots * block_len * width,
        ),
        name="cache_attention",
    )(reqs, live, *queries, cache_key, cache_value)


def tree_kernel(scale, q_ref, kv_ref, tree_ref, out_ref):
    tokens, width = q_ref.shape
    group = min(256, width)
    heads = group // HD
    allowed = jnp.concatenate([tree_ref[...]] * heads, axis=0) > 0.5
    bias = jnp.where(allowed, 0.0, masked_low)
    stats = jnp.zeros((tokens, LANES), jnp.float32)
    for start in range(0, width, group):
        columns = slice(start, start + group)
        queries = block_diagonal(q_ref[:, columns], heads)
        values = kv_ref[:, width + start : width + start + group]
        top, total, out = softmax_parts(queries, kv_ref[:, columns], values, bias, heads, scale)
        out_ref[:, columns] = diagonal_blocks(out, heads, tokens)
        stats = put_stats(stats, start // HD, heads, tokens, top, total)
    out_ref[:, width:] = stats


def tree_attention(queries, key_value, tree, scale):
    tokens, width = queries.shape
    return pl.pallas_call(
        functools.partial(tree_kernel, scale),
        out_shape=jax.ShapeDtypeStruct((tokens, width + LANES), jnp.float32),
        compiler_params=pltpu.CompilerParams(vmem_limit_bytes=8 * 1024 * 1024),
        cost_estimate=pl.CostEstimate(
            flops=16 * tokens * width * tokens, transcendentals=tokens * tokens, bytes_accessed=10**6
        ),
        name="tree_attention",
    )(queries, key_value, tree)


def spread(value, pair, shape):
    lane = lax.broadcasted_iota(jnp.int32, shape, 1)
    first = jnp.broadcast_to(value[:, 2 * pair : 2 * pair + 1], shape)
    second = jnp.broadcast_to(value[:, 2 * pair + 1 : 2 * pair + 2], shape)
    return jnp.where(lane < HD, first, second)


def merged_stats(stats):
    top = functools.reduce(jnp.maximum, stats)
    scales = [jnp.exp(one - top) for one in stats]
    total = sum(one * pltpu.roll(by, HD, axis=1) for one, by in zip(stats, scales))
    return scales, top, total


def merge_kernel(width, finish, *refs):
    *parts, out_ref = refs
    scales, top, total = merged_stats([part[:, width:] for part in parts])
    if finish:
        total = pltpu.roll(total, HD, axis=1)
        scales = [by / total for by in scales]
    else:
        lane = lax.broadcasted_iota(jnp.int32, top.shape, 1)
        out_ref[:, width:] = jnp.where(lane < HD, top, total)
    shape = (top.shape[0], LANES)
    for pair in range(width // LANES):
        columns = slice(pair * LANES, (pair + 1) * LANES)
        out = sum(part[:, columns] * spread(by, pair, shape) for part, by in zip(parts, scales))
        out_ref[:, columns] = out.astype(out_ref.dtype)


def merged(parts, width, finish):
    rows = parts[0].shape[0]
    if finish:
        shape = jax.ShapeDtypeStruct((rows, width), jnp.bfloat16)
    else:
        shape = jax.ShapeDtypeStruct((rows, width + LANES), jnp.float32)
    return pl.pallas_call(
        functools.partial(merge_kernel, width, finish),
        out_shape=shape,
        compiler_params=pltpu.CompilerParams(vmem_limit_bytes=4 * 1024 * 1024),
        cost_estimate=pl.CostEstimate(
            flops=4 * rows * width, transcendentals=rows * LANES, bytes_accessed=12 * rows * width
        ),
        name="merge",
    )(*parts)


def merge(one, two, width):
    return merged([one, two], width, False)


def patch_kernel(rows, reqs, firsts, starts, sel_ref, *refs):
    slots = reqs.shape[0]
    kv_refs = refs[:slots]
    key_ref, value_ref, key_out, value_out, key_buf, value_buf, in_sem, out_sem = refs[slots:]
    tokens = sel_ref.shape[1]
    width = key_ref.shape[2]
    sources, buffers, targets = (key_ref, value_ref), (key_buf, value_buf), (key_out, value_out)

    def window(ref, slot):
        request = reqs[slot]
        return ref.at[request, pl.ds(pl.multiple_of(firsts[request], 16), rows)]

    def fetch(slot, which):
        return pltpu.make_async_copy(
            window(sources[which], slot), buffers[which].at[slot], in_sem.at[slot, which]
        )

    def store(slot, which):
        return pltpu.make_async_copy(
            buffers[which].at[slot], window(targets[which], slot), out_sem.at[slot, which]
        )

    for slot in range(slots):
        for which in range(2):
            fetch(slot, which).start()
    for slot in range(slots):
        request = reqs[slot]
        offset = firsts[request] - starts[request]
        row = lax.broadcasted_iota(jnp.int32, (rows, tokens), 0) + offset
        depth = lax.broadcasted_iota(jnp.int32, (rows, tokens), 1)
        hits = jnp.where(row == depth, 1.0, 0.0).astype(jnp.bfloat16)
        picks = jnp.dot(hits, sel_ref[request], preferred_element_type=jnp.float32)
        touched = jnp.sum(picks, axis=1, keepdims=True) > 0.5
        picks = picks.astype(jnp.bfloat16)
        for which in range(2):
            fresh = kv_refs[slot][:, which * width : (which + 1) * width]
            written = jnp.dot(picks, fresh, preferred_element_type=jnp.float32)
            fetch(slot, which).wait()
            buffer = buffers[which]
            buffer[slot] = jnp.where(touched, written.astype(jnp.bfloat16), buffer[slot])
            store(slot, which).start()
    for slot in range(slots):
        for which in range(2):
            store(slot, which).wait()


def patch(key_values, reqs, selector, starts, keys, values):
    requests, block_len, width = keys.shape
    tokens = selector.shape[1]
    rows = tokens + 16
    firsts = jnp.clip(starts // 16 * 16, 0, block_len - rows)
    vmem = pl.BlockSpec(memory_space=pltpu.VMEM)
    smem = pl.BlockSpec(memory_space=pltpu.SMEM)
    hbm = pl.BlockSpec(memory_space=pltpu.HBM)
    return pl.pallas_call(
        functools.partial(patch_kernel, rows),
        in_specs=[smem] * 3 + [vmem] * (1 + requests) + [hbm] * 2,
        out_specs=[hbm, hbm],
        out_shape=[jax.ShapeDtypeStruct(keys.shape, keys.dtype)] * 2,
        scratch_shapes=[
            pltpu.VMEM((requests, rows, width), keys.dtype),
            pltpu.VMEM((requests, rows, width), keys.dtype),
            pltpu.SemaphoreType.DMA((requests, 2)),
            pltpu.SemaphoreType.DMA((requests, 2)),
        ],
        input_output_aliases={4 + requests: 0, 5 + requests: 1},
        compiler_params=pltpu.CompilerParams(vmem_limit_bytes=8 * 1024 * 1024),
        cost_estimate=pl.CostEstimate(
            flops=0, transcendentals=0, bytes_accessed=8 * requests * rows * width
        ),
        name="patch",
    )(reqs, firsts, starts, selector, *key_values, keys, values)


def on_device(
    hidden,
    w_query,
    w_key,
    w_value,
    w_out,
    cache_key,
    cache_value,
    parents,
    lengths,
    holder,
    selector,
):
    requests, tree_size = parents.shape
    width = w_query.shape[1]
    block_len = cache_key.shape[1]
    block_count = holder.shape[1]
    scale = 1.0 / math.sqrt(HD)
    axis = "blocks"
    index = lax.axis_index(axis)
    levels = requests.bit_length() - 1
    bits = block_count.bit_length() - 1
    assert 1 << levels == requests and 1 << bits == block_count and bits > levels
    split = [1 << s for s in range(levels)]
    whole = [1 << s for s in range(levels, bits)]
    own = sum(((index >> s) & 1) << (levels - 1 - s) for s in range(levels))
    own = own.astype(jnp.int32)
    reqs = own ^ jnp.arange(requests, dtype=jnp.int32)


    def scattered(value):
        for bit in split[1:]:
            middle = value.shape[0] // 2
            value = value[:middle] + swap(value[middle:], axis, bit)
        return value

    def gathered(value):
        values = [value]
        for bit in reversed(split):
            values = values + [swap(one, axis, bit) for one in values]
        return values

    def tied(value, *others):
        return lax.optimization_barrier((value,) + others)

    def after(value, *others):
        return tied(value, *others)[0]

    half = requests // 2 * tree_size
    blocks_of = hidden.reshape(requests, tree_size, -1)
    rows = [lax.dynamic_index_in_dim(blocks_of, own ^ k, 0, False) for k in range(requests)]
    rows = jnp.concatenate(rows, axis=0)

    def first_sum(rows, weights):
        parts = [jnp.dot(rows, w, preferred_element_type=jnp.float32) for w in weights]
        sent = swap(jnp.concatenate([part[half:] for part in parts], axis=1), axis, split[0])
        return jnp.concatenate([part[:half] for part in parts], axis=1) + sent

    query_half = first_sum(rows, [w_query])
    kv_half = first_sum(after(rows, query_half), [w_key, w_value])
    query_sum = scattered(query_half)
    kv_half = after(kv_half, query_sum)
    late_parents, _ = tied(parents, query_sum)
    ancestors = ancestry(lax.dynamic_index_in_dim(late_parents, own, 0, False))
    query_sum = query_sum + swap(query_sum, axis, whole[0])
    query_sum, kv_half, ancestors = tied(query_sum, kv_half, ancestors)
    late_holder = after(holder, query_sum)
    slots = jnp.arange(block_count, dtype=jnp.int32)
    logical = jnp.sum(slots[None, :] * (late_holder == index).astype(jnp.int32), axis=1)
    starts = lengths - logical * block_len
    live = jnp.clip(starts, 0, block_len)
    late_lengths, late_ancestors, _ = tied(lengths, ancestors, query_sum)
    depths = (jnp.sum(late_ancestors, axis=1) - 1.0).astype(jnp.int32)
    positions = lax.dynamic_index_in_dim(late_lengths, own, 0, False) + depths
    tables = rotary_tables(positions)

    kv_sum = scattered(kv_half)
    for bit in whole[1:]:
        query_sum = query_sum + swap(query_sum, axis, bit)
    query_own = rotate(query_sum, tables).astype(jnp.bfloat16)
    queries = gathered(query_own)
    takes_value = (index & whole[0]) > 0
    key_part, value_part = kv_sum[:, :width], kv_sum[:, width:]
    part = jnp.where(takes_value, value_part, key_part)
    part = part + swap(jnp.where(takes_value, key_part, value_part), axis, whole[0])
    *queries, part = tied(*queries, part)

    keep, send, keys_copied, values_copied = cache_attention(
        queries, cache_key, cache_value, reqs, live, scale
    )
    for bit in whole[1:]:
        part = part + swap(part, axis, bit)
    keep, send, part = tied(keep, send, part)
    part = jnp.where(takes_value, part, rotate(part, tables)).astype(jnp.bfloat16)
    far = swap(part, axis, whole[0])
    kv_own = jnp.concatenate(
        [jnp.where(takes_value, far, part), jnp.where(takes_value, part, far)], axis=1
    )
    pieces = [[keep[k]] for k in range(keep.shape[0])]
    arrived = swap(send, axis, split[0])
    for k, piece in enumerate(pieces):
        piece.append(arrived[k])
    for bit in split[1:]:
        middle = len(pieces) // 2
        sent = [merged(piece, width, False) for piece in pieces[middle:]]
        pieces = [piece + [swap(one, axis, bit)] for piece, one in zip(pieces[:middle], sent)]
    cached = merged(pieces[0], width, False)
    for bit in whole[:-1]:
        cached = merge(cached, swap(cached, axis, bit), width)
    tree = tree_attention(query_own, kv_own, ancestors, scale)
    key_out, value_out = patch(
        gathered(kv_own), reqs, selector.astype(jnp.bfloat16), starts, keys_copied, values_copied
    )
    other = swap(cached, axis, whole[-1])
    other, tree = tied(other, tree)
    attended_own = merged([cached, other, tree], width, True)
    everyone = gathered(attended_own)
    everyone[1], key_out, value_out = tied(everyone[1], key_out, value_out)

    mixed = [jnp.dot(one, w_out, preferred_element_type=jnp.float32) for one in everyone]
    natural = []
    for request in range(requests):
        row = mixed[0]
        for k in range(1, requests):
            row = jnp.where(own == request ^ k, mixed[k], row)
        natural.append(row)
    mixed = jnp.concatenate(natural, axis=0)
    head_bit = lax.axis_size("heads") // 2
    while head_bit:
        high = (lax.axis_index("heads") & head_bit) > 0
        middle = mixed.shape[0] // 2
        kept = jnp.where(high, mixed[middle:], mixed[:middle])
        sent = jnp.where(high, mixed[:middle], mixed[middle:])
        mixed = kept + swap(sent, "heads", head_bit)
        head_bit //= 2
    mixed = mixed.astype(jnp.bfloat16)

    return (mixed, key_out, value_out)


def solution(mesh):
    return jax.shard_map(
        on_device,
        mesh=mesh,
        in_specs=(
            P(None, "blocks"),
            P("blocks", "heads"),
            P("blocks", "heads"),
            P("blocks", "heads"),
            P("heads", "blocks"),
            P(None, "blocks", "heads"),
            P(None, "blocks", "heads"),
            P(),
            P(),
            P(),
            P(),
        ),
        out_specs=(P("heads", "blocks"), P(None, "blocks", "heads"), P(None, "blocks", "heads")),
        check_vma=False,
    )
```
